32 devices in a mesh: tm: 8 (over z, y), space: 4 (over x, core).
Axes of the slice: x: 2, y: 2, z: 4, core: 2. Of those that a mesh axis runs over, the one named last changes fastest.
Arguments:
- attn_query: bfloat16 [4096, 2560], P(('tm', 'space')), may hold values from -8 to 8
- attn_key: bfloat16 [4096, 2560], P(('tm', 'space')), may hold values from -8 to 8
- attn_value: bfloat16 [4096, 2560], P(('tm', 'space')), may hold values from -6 to 6
- attn_outgrad: bfloat16 [4096, 2560], P(('tm', 'space')), may hold values from -6 to 6
- fast_query: bfloat16 [4096, 1536], P('tm'), may hold values from -6 to 6
- fast_outgrad: bfloat16 [4096, 1536], P('tm'), may hold values from -6 to 6
- fast_key: bfloat16 [4096, 1536], P('tm'), may hold values from -6 to 6
- gate_weights: bfloat16 [8, 1536, 3072], P('tm', None, 'space'), may hold values from -0.15625 to 0.15625
- up_weights: bfloat16 [8, 1536, 3072], P('tm', None, 'space'), may hold values from -0.15625 to 0.15625
- down_weights: bfloat16 [8, 3072, 1536], P('tm', 'space'), may hold values from -0.109375 to 0.109375
- gate_factor: bfloat16 [4096, 3072], P('tm', 'space'), may hold values from -0.15625 to 0.15625
- clip_groups: int32 [4], replicated, may hold values from 1 to 4, 8 in all
Outputs:
- query_grad: bfloat16 [4096, 2560], P(('tm', 'space'))
- key_grad: bfloat16 [4096, 2560], P(('tm', 'space'))
- value_grad: bfloat16 [4096, 2560], P(('tm', 'space'))
- fast_grad: bfloat16 [4096, 1536], P(('tm', 'space'))
- rate_grad: float32 [4096], P(('tm', 'space'))
The draws below stay inside these ranges and needn't reach their ends.
Inputs may be any that keep to these rules, and one draw needn't show every extreme that they name: `clip_groups`: clip k covers the groups after those of clips 0 to k - 1; the counts sum to 8.
All inputs are finite; a program needn't handle non-finite values.
Results may differ from the reference program's by a relative error of at most 0.012.
Values may be sent and summed in bfloat16 or wider, within the bound.
No kernel may reach another device: no remote copies, remote signals or barrier semaphores. Data moves between devices by JAX's collectives and lax.ppermute only.
A program may use at most 192 MiB of HBM per device.

```python
import math
import jax
import jax.numpy as jnp
import numpy as np
from jax import lax

HEAD = 128
FD = 1536
FH = 3072
NCLIPS = 4
TILE = 128
D = 2560
REACH = 64
ROWS = 512
GROUPS = 8
TOTAL = 4096
MOST = 4
N_SPACE = 4


def paired_rows(key):
    base = jax.random.fold_in(key, 7)
    first_key, second_key = jax.random.split(base, 2)
    queries = jnp.clip(jax.random.normal(first_key, (TOTAL, D), jnp.float32), -6.0, 6.0)
    keys_drawn = jnp.clip(jax.random.normal(second_key, (TOTAL, D), jnp.float32), -6.0, 6.0)
    return (queries, keys_drawn)


def draw_attn_query(key, part):
    return paired_rows(key)[0].astype(jnp.bfloat16)


def draw_attn_key(key, part):
    return paired_rows(key)[1].astype(jnp.bfloat16)


def steps_of(own_key, extent, cuts, smallest, high):
    level = 1.0
    for dim, parts in cuts:
        heights = jax.random.uniform(jax.random.fold_in(jax.random.fold_in(own_key, 6), dim), (parts,), jnp.float32, smallest / len(cuts), high / len(cuts))
        level = level * jnp.repeat(jnp.exp(heights), extent[dim] // parts).reshape((-1,) + (1,) * (len(extent) - 1 - dim))
    return level


def split_up(number_of, total, reach, skew):
    weights = [(1 << 20) // math.isqrt(rank ** skew) + 1 for rank in range(2, number_of + 1)]
    rest, holding = total - reach - (number_of - 1), [1] * (number_of - 1)
    while rest > 0:
        movable = [i for i in range(number_of - 1) if holding[i] < reach]
        mass, budget = sum([weights[i] for i in movable]), rest
        for i in movable:
            extra = min(reach - holding[i], max(1, budget * weights[i] // mass), rest)
            holding[i] = holding[i] + extra
            rest = rest - extra
    return np.array([reach] + holding)


def ragged(stream_key, amount, total, reach, lean):
    if amount == 2:
        one = jax.random.randint(stream_key, (), max(1, total - reach), min(reach, total - 1) + 1)
        return jnp.stack([one, total - one])
    sizes = jnp.asarray(split_up(amount, total, reach, lean), jnp.int32)
    twos = (amount - 1) // 2
    source_of, sink = sizes[1:1 + 2 * twos:2], sizes[2:2 + 2 * twos:2]
    slack = jnp.minimum(source_of - 1, reach - sink)
    passed = jax.random.randint(jax.random.fold_in(stream_key, 1), (twos,), 0, 1 << 20) % (slack + 1)
    sizes = sizes.at[1:1 + 2 * twos:2].set(source_of - passed).at[2:2 + 2 * twos:2].set(sink + passed)
    return sizes[jax.random.permutation(jax.random.fold_in(stream_key, 2), amount)]


def scatter_about(own_key, extent, scale, reach, shards=(), held_as=jnp.bfloat16):
    factor_of = steps_of(own_key, extent, shards, -0.22, 0.18) if shards else 1.0
    entries = jax.random.normal(own_key, extent, jnp.float32) * scale * factor_of
    return jnp.minimum(jnp.maximum(entries, -reach), reach).astype(held_as)


def setup_inputs(seed: int = 0) -> dict:
    splits = jax.random.split(jax.random.key(seed), 13)
    return {
        "attn_query": draw_attn_query(jax.random.fold_in(splits[12], 71), 0),
        "attn_key": draw_attn_key(jax.random.fold_in(splits[12], 71), 0),
        "attn_value": scatter_about(splits[2], (TOTAL, D), 1.0, 6.0, ((0, 32),)),
        "attn_outgrad": scatter_about(splits[3], (TOTAL, D), 1.0, 6.0, ((0, 32),)),
        "fast_query": scatter_about(splits[4], (TOTAL, FD), 1.0, 6.0, ((0, 8),)),
        "fast_outgrad": scatter_about(splits[5], (TOTAL, FD), 1.0, 6.0, ((0, 8),)),
        "fast_key": scatter_about(splits[6], (TOTAL, FD), 1.0, 6.0, ((0, 8),)),
        "gate_weights": scatter_about(splits[7], (GROUPS, FD, FH), FD ** -0.5, 0.15625, ((0, 8), (2, 4))),
        "up_weights": scatter_about(splits[8], (GROUPS, FD, FH), FD ** -0.5, 0.15625, ((0, 8), (2, 4))),
        "down_weights": scatter_about(splits[9], (GROUPS, FH, FD), FH ** -0.5, 0.109375, ((0, 8), (1, 4))),
        "gate_factor": scatter_about(splits[10], (TOTAL, FH), FD ** -0.5, 0.15625, ((0, 8), (1, 4))),
        "clip_groups": ragged(splits[11], NCLIPS, GROUPS, MOST, 2).astype(jnp.int32),
    }


def window_grads(queries, key_rows, value_rows, out_grad, query_pos, key_pos, key_live):
    head_count = queries.shape[1] // HEAD
    query_heads = queries.astype(jnp.float32).reshape(queries.shape[0], head_count, HEAD)
    key_heads = key_rows.astype(jnp.float32).reshape(key_rows.shape[0], head_count, HEAD)
    value_heads = value_rows.astype(jnp.float32).reshape(value_rows.shape[0], head_count, HEAD)
    grad_heads = out_grad.astype(jnp.float32).reshape(out_grad.shape[0], head_count, HEAD)
    scaling = 1.0 / math.sqrt(HEAD)
    scores = jnp.einsum('qhd,khd->hqk', query_heads, key_heads) * scaling
    allowed = key_live[None, :] & (jnp.abs(query_pos[:, None] - key_pos[None, :]) <= REACH)
    scores = jnp.where(allowed[None], scores, -1e+30)
    peak_score = lax.optimization_barrier(jnp.max(scores, axis=2, keepdims=True))
    exponent = jnp.exp(scores - peak_score)
    attn_weights = exponent / lax.optimization_barrier(jnp.sum(exponent, axis=2, keepdims=True))
    weights_b = lax.optimization_barrier(attn_weights.astype(jnp.bfloat16)).astype(jnp.float32)
    attn_out = jnp.einsum('hqk,khd->qhd', weights_b, value_heads)
    row_delta = lax.optimization_barrier(jnp.sum(grad_heads * attn_out, axis=2))
    value_grad = jnp.einsum('hqk,qhd->khd', weights_b, grad_heads)
    weight_grad = jnp.einsum('qhd,khd->hqk', grad_heads, value_heads)
    score_grad = attn_weights * (weight_grad - jnp.transpose(row_delta)[:, :, None])
    score_grad_b = lax.optimization_barrier(score_grad.astype(jnp.bfloat16)).astype(jnp.float32)
    query_grad = jnp.einsum('hqk,khd->qhd', score_grad_b, key_heads) * scaling
    key_grad = jnp.einsum('hqk,qhd->khd', score_grad_b, query_heads) * scaling
    return (query_grad.reshape(queries.shape[0], -1), key_grad.reshape(key_rows.shape[0], -1), value_grad.reshape(value_rows.shape[0], -1))

def assemble(extended):
    blocks = extended.reshape(GROUPS, N_SPACE, TILE + 2 * REACH, D)
    middle = blocks[:, :, REACH:REACH + TILE]
    from_left = jnp.pad(blocks[:, :-1, TILE + REACH:], ((0, 0), (1, 0), (0, TILE - REACH), (0, 0)))
    from_right = jnp.pad(blocks[:, 1:, :REACH], ((0, 0), (0, 1), (TILE - REACH, 0), (0, 0)))
    return (middle + from_left + from_right).reshape(TOTAL, D).astype(jnp.bfloat16)

def reference(attn_query, attn_key, attn_value, attn_outgrad, fast_query, fast_outgrad, fast_key, gate_weights, up_weights, down_weights, gate_factor, clip_groups):
    tile_count = GROUPS * N_SPACE
    query_tiles = attn_query.reshape(tile_count, TILE, D)
    grad_tiles = attn_outgrad.reshape(tile_count, TILE, D)
    key_pad = jnp.pad(attn_key.reshape(GROUPS, ROWS, D), ((0, 0), (REACH, REACH), (0, 0)))
    value_pad = jnp.pad(attn_value.reshape(GROUPS, ROWS, D), ((0, 0), (REACH, REACH), (0, 0)))

    def per_tile(inputs):
        queries, out_grad, index = inputs
        group = index // N_SPACE
        start = (index % N_SPACE * TILE).astype(jnp.int32)
        key_rows = lax.dynamic_slice_in_dim(lax.dynamic_index_in_dim(key_pad, group, 0, False), start, TILE + 2 * REACH, 0)
        value_rows = lax.dynamic_slice_in_dim(lax.dynamic_index_in_dim(value_pad, group, 0, False), start, TILE + 2 * REACH, 0)
        query_pos = start + jnp.arange(TILE, dtype=jnp.int32)
        key_pos = start - REACH + jnp.arange(TILE + 2 * REACH, dtype=jnp.int32)
        key_live = (key_pos >= 0) & (key_pos < ROWS)
        return window_grads(queries, key_rows, value_rows, out_grad, query_pos, key_pos, key_live)
    query_all, key_ext, value_ext = lax.map(per_tile, (query_tiles, grad_tiles, jnp.arange(tile_count, dtype=jnp.int32)))
    query_grad = query_all.reshape(TOTAL, D).astype(jnp.bfloat16)
    key_grad = assemble(key_ext)
    value_grad = assemble(value_ext)
    starts = jnp.cumsum(clip_groups) - clip_groups
    first = jnp.any(starts[None, :] == jnp.arange(GROUPS, dtype=jnp.int32)[:, None], axis=1).astype(jnp.float32)
    contract_rows = (((0,), (0,)), ((), ()))
    contract_last = (((1,), (1,)), ((), ()))

    def backward_step(gate_carry, inputs):
        queries, out_grad, key_rows, gate_w, up_w, down_w, gate_f, flag = inputs
        gate_pre = jnp.dot(queries, gate_w, preferred_element_type=jnp.float32)
        up_pre = jnp.dot(queries, up_w, preferred_element_type=jnp.float32)
        gate_sig = jax.nn.sigmoid(gate_pre)
        gate_act = gate_pre * gate_sig
        hidden_grad = lax.dot_general(out_grad, down_w, contract_last, preferred_element_type=jnp.float32)
        gate_grad_b = (hidden_grad * up_pre * gate_sig * (1.0 + gate_pre * (1.0 - gate_sig))).astype(jnp.bfloat16)
        up_grad_b = (hidden_grad * gate_act).astype(jnp.bfloat16)
        input_grad = lax.dot_general(gate_grad_b, gate_w, contract_last, preferred_element_type=jnp.float32) + lax.dot_general(up_grad_b, up_w, contract_last, preferred_element_type=jnp.float32)
        rate = lax.optimization_barrier(jnp.sum(jnp.dot(key_rows, gate_carry.astype(jnp.bfloat16), preferred_element_type=jnp.float32) * gate_f, axis=1)) / ROWS
        gate_total = lax.dot_general(queries, gate_grad_b, contract_rows, preferred_element_type=jnp.float32)
        renewed = (1.0 - flag) * (gate_carry + gate_total)
        return (renewed, (input_grad.astype(jnp.bfloat16), rate))
    initial = jnp.zeros((FD, FH), jnp.float32)
    inputs = (fast_query.reshape(GROUPS, ROWS, FD), fast_outgrad.reshape(GROUPS, ROWS, FD), fast_key.reshape(GROUPS, ROWS, FD), gate_weights, up_weights, down_weights, gate_factor.reshape(GROUPS, ROWS, FH), first)
    ending, outputs = lax.scan(backward_step, initial, inputs, reverse=True)
    fast_grad = outputs[0].reshape(TOTAL, FD)
    rate_grad = outputs[1].reshape(TOTAL)
    return (query_grad, key_grad, value_grad, fast_grad, rate_grad)
```

```python
import functools
import math

import jax
import jax.numpy as jnp
from jax import lax
from jax.experimental import pallas as pl
from jax.experimental.pallas import tpu as pltpu
from jax.sharding import PartitionSpec as P

HEAD = 128

CONTRACT_LAST = (((1,), (1,)), ((), ()))
CONTRACT_FIRST = (((0,), (0,)), ((), ()))
F32 = jnp.float32
BF16 = jnp.bfloat16


def dot_last(a, b):
    return lax.dot_general(a, b, CONTRACT_LAST, preferred_element_type=F32)


def cost(flops, moved, transcendentals=0):
    return pl.CostEstimate(flops=flops, bytes_accessed=moved, transcendentals=transcendentals)


def attention_kernel(reach, last, scal, q, g, k, v, hc, hx, dq, own, mc, mx):
    rows = q.shape[0]
    keys = rows + 2 * reach
    at = scal[1]
    even = at % 2 == 0
    scaling = 1.0 / math.sqrt(HEAD)
    key_row = lax.broadcasted_iota(jnp.int32, (keys, rows), 0)
    query_row = lax.broadcasted_iota(jnp.int32, (keys, rows), 1)
    shift_c = jnp.where(even, 0, -(rows + reach))
    shift_x = jnp.where(even, -(rows + 2 * reach), -reach)
    key_pos = key_row + jnp.where(
        key_row < rows, 0, jnp.where(key_row < rows + reach, shift_c, shift_x)
    )
    offset = at * rows
    live = (key_pos + offset >= 0) & (key_pos + offset < last)
    allowed = live & (jnp.abs(key_pos - query_row) <= reach)
    for h in range(q.shape[1] // HEAD):
        col = slice(h * HEAD, (h + 1) * HEAD)
        qh, gh = q[:, col], g[:, col]
        kh = jnp.concatenate([k[:, col], hc[0, :, col], hx[0, :, col]], axis=0)
        vh = jnp.concatenate([v[:, col], hc[1, :, col], hx[1, :, col]], axis=0)
        scores = jnp.where(allowed, dot_last(kh, qh) * scaling, -1e30)
        exponent = jnp.exp(scores - jnp.max(scores, axis=0, keepdims=True))
        probs = exponent * (1.0 / jnp.sum(exponent, axis=0, keepdims=True))
        probs_b = probs.astype(BF16)
        dprobs = dot_last(vh, gh)
        delta = jnp.sum(probs_b.astype(F32) * dprobs, axis=0, keepdims=True)
        dscores_b = (probs * (dprobs - delta)).astype(BF16)
        dv = jnp.dot(probs_b, gh, preferred_element_type=F32)
        dk = jnp.dot(dscores_b, qh, preferred_element_type=F32) * scaling
        dqh = lax.dot_general(dscores_b, kh, CONTRACT_FIRST, preferred_element_type=F32)
        dq[:, col] = (dqh * scaling).astype(BF16)
        for i, grad in enumerate((dk, dv)):
            own[i, :, col] = grad[:rows]
            mc[i, :, col] = grad[rows : rows + reach].astype(BF16)
            mx[i, :, col] = grad[rows + reach :].astype(BF16)


def attention(scal, query, out_grad, key, value, halo_c, halo_x, last):
    rows, width = query.shape
    reach = halo_c.shape[1]
    heads = width // HEAD
    step = next(s for s in (4, 2, 1) if heads % s == 0) * HEAD
    flat = pl.BlockSpec((rows, step), lambda i: (0, i))
    half = pl.BlockSpec((2, reach, step), lambda i: (0, 0, i))
    both = pl.BlockSpec((2, rows, step), lambda i: (0, 0, i))
    keys = rows + 2 * reach
    return pl.pallas_call(
        functools.partial(attention_kernel, reach, last),
        grid=(width // step,),
        in_specs=[pl.BlockSpec(memory_space=pltpu.SMEM), flat, flat, flat, flat, half, half],
        out_specs=[flat, both, half, half],
        out_shape=[
            jax.ShapeDtypeStruct((rows, width), BF16),
            jax.ShapeDtypeStruct((2, rows, width), F32),
            jax.ShapeDtypeStruct((2, reach, width), BF16),
            jax.ShapeDtypeStruct((2, reach, width), BF16),
        ],
        cost_estimate=cost(
            12 * rows * keys * width, 2 * width * (12 * rows), heads * rows * keys
        ),
        name="window_attention",
    )(scal, query, out_grad, key, value, halo_c, halo_x)


def scores_kernel(scal, k0, ka, kb, q0, *refs):
    halves, out = refs[:-1], refs[-1]
    half = ka.shape[0]
    odd = scal[1] % 2
    first = pl.multiple_of(odd * half, half)
    second = pl.multiple_of((1 - odd) * half, half)
    everywhere = slice(None)

    def put(pair, r, q, i, k):
        out[pair, r, i] = dot_last(q[...], k[...]).astype(BF16)

    for k, i in ((ka, first), (kb, second)):
        put(0, everywhere, q0, pl.ds(i, half), k)
    for n in range(len(halves) // 2):
        for q, r in zip(halves[2 * n : 2 * n + 2], (first, second)):
            put(2 * n + 1, pl.ds(r, half), q, everywhere, k0)
            for k, i in ((ka, first), (kb, second)):
                put(2 * n + 2, pl.ds(r, half), q, pl.ds(i, half), k)


def scores(scal, k0, ka, kb, q0, halves):
    rows, width = k0.shape
    pairs = 1 + len(halves)
    vmem = pl.BlockSpec(memory_space=pltpu.VMEM)
    return pl.pallas_call(
        scores_kernel,
        in_specs=[pl.BlockSpec(memory_space=pltpu.SMEM)] + [vmem] * (4 + len(halves)),
        out_specs=vmem,
        out_shape=jax.ShapeDtypeStruct((pairs, rows, rows), BF16),
        cost_estimate=cost(
            2 * pairs * rows * rows * width, 2 * (pairs * rows * rows + (2 + pairs) * rows * width)
        ),
        name="pair_scores",
    )(scal, k0, ka, kb, q0, *halves)


def rates_kernel(shifts, scal, clips, f0, f1, st, g0, *refs):
    moved, out = refs[:-1], refs[-1]
    at = scal[0]
    starts, total = [], 0
    for n in range(clips.shape[0]):
        starts.append(total)
        total = total + clips[n]

    def together(u, v):
        apart = jnp.bool_(False)
        for x in range(1 - u, v + 1):
            for start in starts:
                apart = apart | (start == at + x)
        return jnp.where(apart, 0.0, 1.0)

    share = 1.0 / st.shape[1]

    def pair(n, g, f, u, v):
        products = dot_last(g[...], f[...])
        summed = jnp.sum(st[n].astype(F32) * products, axis=0, keepdims=True)
        return summed * (together(u, v) * share)

    before = pair(0, g0, f1, 1, 0)
    own = jnp.zeros_like(before)
    for n, (g, v) in enumerate(zip(moved, shifts)):
        own += pair(2 * n + 1, g, f0, 0, v)
        before += pair(2 * n + 2, g, f1, 1, v)
    lanes = out.shape[2]
    for n in range(out.shape[0]):
        part = slice(n * lanes, (n + 1) * lanes)
        out[n, 0:1, :] = own[:, part]
        out[n, 1:2, :] = before[:, part]


def rates(scal, clips, f0, f1, st, g0, moved, shifts, tiles):
    rows, width = f0.shape
    pairs = st.shape[0]
    step = rows // 2
    smem = pl.BlockSpec(memory_space=pltpu.SMEM)
    vmem = pl.BlockSpec(memory_space=pltpu.VMEM)
    factor = pl.BlockSpec((step, width), lambda i: (i, 0))
    return pl.pallas_call(
        functools.partial(rates_kernel, shifts),
        grid=(2,),
        in_specs=[
            smem,
            smem,
            factor,
            factor,
            pl.BlockSpec((pairs, rows, step), lambda i: (0, 0, i)),
        ]
        + [vmem] * (1 + len(moved)),
        out_specs=pl.BlockSpec((tiles // 2, 2, rows // tiles), lambda i: (i, 0, 0)),
        out_shape=jax.ShapeDtypeStruct((tiles, 2, rows // tiles), F32),
        cost_estimate=cost(
            2 * pairs * rows * rows * width, 2 * (pairs * rows * rows + (2 + pairs) * rows * width)
        ),
        name="pair_rates",
    )(scal, clips, f0, f1, st, g0, *moved)


def shifted(array, axis, by):
    devices = lax.axis_size(axis)
    pairs = [(i + by, i) for i in range(devices) if 0 <= i + by < devices]
    return lax.ppermute(array, axis, pairs)


def swapped(array, axis, first):
    devices = lax.axis_size(axis)
    pairs = [(i, i + 1) for i in range(first, devices - 1, 2)]
    return lax.ppermute(array, axis, pairs + [(j, i) for i, j in pairs])


def per_device(
    attn_query,
    attn_key,
    attn_value,
    attn_outgrad,
    fast_query,
    fast_outgrad,
    fast_key,
    gate_weights,
    up_weights,
    down_weights,
    gate_factor,
    clip_groups,
):
    groups, tiles = lax.axis_size("tm"), lax.axis_size("space")
    group, tile = lax.axis_index("tm"), lax.axis_index("space")
    scal = jnp.stack([group, tile]).astype(jnp.int32)
    odd = tile % 2
    rows = fast_query.shape[0]
    half = rows // 2
    tile_rows, width = attn_query.shape
    reach = tile_rows // 2
    most = groups // 2
    shifts = tuple(range(2, most, 2))

    key_half = lax.dynamic_slice_in_dim(fast_key, odd * half, half, 0)
    query_half = lax.dynamic_slice_in_dim(fast_query, odd * half, half, 0)
    key_first = shifted(key_half, "tm", -1)
    query_first = [shifted(query_half, "tm", v) for v in shifts]
    stacked = jnp.stack([attn_key, attn_value]).reshape(2, 2, reach, width)
    halo_x = swapped(lax.dynamic_index_in_dim(stacked, odd, 1, False), "space", 1)
    halo_c = swapped(lax.dynamic_index_in_dim(stacked, 1 - odd, 1, False), "space", 0)
    factor_before = shifted(gate_factor, "tm", -1)

    gate_w, up_w, down_w = gate_weights[0], up_weights[0], down_weights[0]
    gate_pre = jnp.dot(fast_query, gate_w, preferred_element_type=F32)
    up_pre = jnp.dot(fast_query, up_w, preferred_element_type=F32)
    gate_sig = jax.nn.sigmoid(gate_pre)
    hidden_grad = dot_last(fast_outgrad, down_w)
    gate_grad_b = (hidden_grad * up_pre * gate_sig * (1.0 + gate_pre * (1.0 - gate_sig))).astype(
        BF16
    )
    moved = [shifted(gate_grad_b, "tm", v) for v in shifts]
    up_grad_b = (hidden_grad * (gate_pre * gate_sig)).astype(BF16)

    query_grad, own, margin_c, margin_x = attention(
        scal, attn_query, attn_outgrad, attn_key, attn_value, halo_c, halo_x, rows
    )
    margin_x = swapped(margin_x, "space", 1)
    margin_c = swapped(margin_c, "space", 0)

    input_part = dot_last(gate_grad_b, gate_w) + dot_last(up_grad_b, up_w)
    parts = input_part.astype(BF16).reshape(tiles, tile_rows, -1)
    parts = lax.all_to_all(parts, "space", 0, 0)
    fast_grad = jnp.sum(parts.astype(F32), axis=0).astype(BF16)

    key_second = swapped(key_first, "space", 0)
    halves = []
    for part in query_first:
        halves += [part, swapped(part, "space", 0)]
    st = scores(scal, fast_key, key_first, key_second, fast_query, halves)
    rate = rates(
        scal, clip_groups, gate_factor, factor_before, st, gate_grad_b, moved, shifts, tiles
    )
    rate = jnp.sum(lax.all_to_all(rate, "space", 0, 0), axis=0)
    rate_grad = rate[0] + shifted(rate[1], "tm", 1)

    from_even = jnp.where(odd == 0, margin_x, margin_c)
    from_odd = jnp.where(odd == 0, margin_c, margin_x)
    summed = own + jnp.concatenate([from_even, from_odd], axis=1).astype(F32)
    return (
        query_grad,
        summed[0].astype(BF16),
        summed[1].astype(BF16),
        fast_grad,
        rate_grad,
    )


def solution(mesh):
    over = ("tm", "space")
    tiled = P(over, None)
    in_specs = (
        (tiled,) * 4
        + (P("tm", None),) * 3
        + (P("tm", None, "space"),) * 2
        + (P("tm", "space", None), P("tm", "space"), P())
    )
    return jax.shard_map(
        per_device,
        mesh=mesh,
        in_specs=in_specs,
        out_specs=(tiled,) * 4 + (P(over),),
        check_vma=False,
    )
```

```python
import functools
import math

import jax
import jax.numpy as jnp
from jax import lax
from jax.experimental import pallas as pl
from jax.experimental.pallas import tpu as pltpu
from jax.sharding import PartitionSpec as P


HEAD = 128

CONTRACT_LAST = (((1,), (1,)), ((), ()))
CONTRACT_FIRST = (((0,), (0,)), ((), ()))
F32 = jnp.float32
BF16 = jnp.bfloat16


def dot_last(a, b):
    return lax.dot_general(a, b, CONTRACT_LAST, preferred_element_type=F32)


def cost(flops, moved, transcendentals=0):
    return pl.CostEstimate(flops=flops, bytes_accessed=moved, transcendentals=transcendentals)


def pick_kernel(scal, fk, fq, k, v, out, hc, hx, sems):
    reach = hc.shape[1]
    odd = scal[1] % 2
    first = pltpu.make_async_copy(fk, out, sems.at[0])

    @pl.when(odd == 0)
    def _():
        first.start()

    @pl.when(odd == 1)
    def _():
        pltpu.make_async_copy(fq, out, sems.at[0]).start()

    copies = []
    for i, source in enumerate((k, v)):
        for j, (half, at) in enumerate(((hx, odd), (hc, 1 - odd))):
            rows = pl.ds(pl.multiple_of(at * reach, reach), reach)
            copies.append(pltpu.make_async_copy(source.at[rows], half.at[i], sems.at[1 + 2 * i + j]))
    for copy in copies:
        copy.start()
    first.wait()
    for copy in copies:
        copy.wait()


def pick(scal, fast_key, fast_query, key, value):
    rows, width = key.shape
    half = jax.ShapeDtypeStruct((2, rows // 2, width), BF16)
    return pl.pallas_call(
        pick_kernel,
        in_specs=[pl.BlockSpec(memory_space=pltpu.SMEM)]
        + [pl.BlockSpec(memory_space=pl.ANY)] * 4,
        out_specs=[pl.BlockSpec(memory_space=pltpu.VMEM)] * 3,
        out_shape=[jax.ShapeDtypeStruct(fast_key.shape, BF16), half, half],
        scratch_shapes=[pltpu.SemaphoreType.DMA((5,))],
        cost_estimate=cost(0, 4 * fast_key.size + 8 * rows * width),
        name="pick_outgoing",
    )(scal, fast_key, fast_query, key, value)


def weights_kernel(shifts, scal, clips, out):
    at = scal[0]
    starts, total = [], 0
    for n in range(clips.shape[0]):
        starts.append(total)
        total = total + clips[n]

    def together(u, v):
        apart = jnp.bool_(False)
        for x in range(1 - u, v + 1):
            for start in starts:
                apart = apart | (start == at + x)
        return jnp.where(apart, 0.0, 1.0)

    for n, (u, v) in enumerate([(1, 0)] + [(u, v) for v in shifts for u in (0, 1)]):
        out[n : n + 1, :] = jnp.full((1, out.shape[1]), together(u, v), F32)


def pair_weights(scal, clips, shifts):
    return pl.pallas_call(
        functools.partial(weights_kernel, shifts),
        in_specs=[pl.BlockSpec(memory_space=pltpu.SMEM)] * 2,
        out_specs=pl.BlockSpec(memory_space=pltpu.VMEM),
        out_shape=jax.ShapeDtypeStruct((1 + 2 * len(shifts), HEAD), F32),
        cost_estimate=cost(20 * 10**9, 4096),
        compiler_params=pltpu.CompilerParams(vmem_limit_bytes=1 << 20),
        name="pair_weights",
    )(scal, clips)


def fast_kernel(step, q, og, gw, uw, dw, gate_out, part_out, gate_grad, up_grad, part, sems):
    for j in range(gw.shape[2] // step):
        cols = slice(j * step, (j + 1) * step)
        gate = jnp.dot(q[...], gw[0, :, cols], preferred_element_type=F32)
        up = jnp.dot(q[...], uw[0, :, cols], preferred_element_type=F32)
        hidden = dot_last(og[...], dw[0, cols, :])
        sig = jax.nn.sigmoid(gate)
        gate_grad[:, cols] = (hidden * up * sig * (1.0 + gate * (1.0 - sig))).astype(BF16)
        up_grad[:, cols] = (hidden * (gate * sig)).astype(BF16)
    copies = [pltpu.make_async_copy(gate_grad, gate_out, sems.at[0])]
    copies[0].start()
    for j in range(q.shape[1] // step):
        rows = slice(j * step, (j + 1) * step)
        part[:, rows] = (
            dot_last(gate_grad[...], gw[0, rows, :]) + dot_last(up_grad[...], uw[0, rows, :])
        ).astype(BF16)
        copy = pltpu.make_async_copy(part.at[:, rows], part_out.at[:, rows], sems.at[1 + j])
        copy.start()
        copies.append(copy)
    for copy in copies:
        copy.wait()


def fast(query, outgrad, gate_w, up_w, down_w):
    rows, width = query.shape
    hidden = gate_w.shape[2]
    step = next(s for s in (256, 128) if hidden % s == 0 and width % s == 0)
    vmem = pl.BlockSpec(memory_space=pltpu.VMEM)
    return pl.pallas_call(
        functools.partial(fast_kernel, step),
        in_specs=[vmem] * 5,
        out_specs=[pl.BlockSpec(memory_space=pltpu.HBM)] * 2,
        out_shape=[
            jax.ShapeDtypeStruct((rows, hidden), BF16),
            jax.ShapeDtypeStruct((rows, width), BF16),
        ],
        scratch_shapes=[
            pltpu.VMEM((rows, hidden), BF16),
            pltpu.VMEM((rows, hidden), BF16),
            pltpu.VMEM((rows, width), BF16),
            pltpu.SemaphoreType.DMA((1 + width // step,)),
        ],
        cost_estimate=cost(20 * 10**9, 6 * width * hidden + 8 * rows * width),
        compiler_params=pltpu.CompilerParams(vmem_limit_bytes=26 << 20),
        name="fast_weights",
    )(query, outgrad, gate_w, up_w, down_w)


def attention_kernel(reach, last, every, scal, q, g, k, v, hc, hx, *refs):
    outs, held, sems = refs[:5], refs[5:10], refs[10]
    dq, dk_own, dv_own, mc, mx = held
    copies = []
    rows = q.shape[0]
    keys = rows + 2 * reach
    wide = 2 * HEAD
    at = scal[1]
    even = at % 2 == 0
    scaling = 1.0 / math.sqrt(HEAD)
    key_row = lax.broadcasted_iota(jnp.int32, (keys, rows), 0)
    query_row = lax.broadcasted_iota(jnp.int32, (keys, rows), 1)
    shift_c = jnp.where(even, 0, -(rows + reach))
    shift_x = jnp.where(even, -(rows + 2 * reach), -reach)
    key_pos = key_row + jnp.where(
        key_row < rows, 0, jnp.where(key_row < rows + reach, shift_c, shift_x)
    )
    offset = at * rows
    live = (key_pos + offset >= 0) & (key_pos + offset < last)
    bias = jnp.where(live & (jnp.abs(key_pos - query_row) <= reach), 0.0, -1e30)
    bias = jnp.concatenate([bias, bias], axis=1)
    zero = jnp.zeros((rows, HEAD), BF16)

    def diagonal(ref, at):
        head, other = ref[:, at : at + HEAD], ref[:, at + HEAD : at + wide]
        return jnp.concatenate(
            [jnp.concatenate([head, zero], axis=1), jnp.concatenate([zero, other], axis=1)], axis=0
        )

    for start in range(0, q.shape[1], wide):
        col = slice(start, start + wide)
        kk = jnp.concatenate([k[:, col], hc[0, :, col], hx[0, :, col]], axis=0)
        vv = jnp.concatenate([v[:, col], hc[1, :, col], hx[1, :, col]], axis=0)
        qd, gd = diagonal(q, start), diagonal(g, start)
        scores = dot_last(kk, qd) * scaling + bias
        exponent = jnp.exp(scores - jnp.max(scores, axis=0, keepdims=True))
        probs = exponent * (1.0 / jnp.sum(exponent, axis=0, keepdims=True))
        probs_b = probs.astype(BF16)
        dprobs = dot_last(vv, gd)
        delta = jnp.sum(probs_b.astype(F32) * dprobs, axis=0, keepdims=True)
        dscores_b = (probs * (dprobs - delta)).astype(BF16)
        dv = jnp.dot(probs_b, gd, preferred_element_type=F32)
        dk = jnp.dot(dscores_b, qd, preferred_element_type=F32) * scaling
        both = lax.dot_general(dscores_b, kk, CONTRACT_FIRST, preferred_element_type=F32)
        dq[:, start : start + HEAD] = (both[:rows, :HEAD] * scaling).astype(BF16)
        dq[:, start + HEAD : start + wide] = (both[rows:, HEAD:] * scaling).astype(BF16)
        for i, (grad, own) in enumerate(((dk, dk_own), (dv, dv_own))):
            own[:, col] = grad[:rows].astype(BF16)
            mc[i, :, col] = grad[rows : rows + reach].astype(BF16)
            mx[i, :, col] = grad[rows + reach :].astype(BF16)
        if (start + wide) % every == 0:
            done = (Ellipsis, slice(start + wide - every, start + wide))
            for i, (ref, out) in enumerate(zip(held, outs)):
                sem = sems.at[start // every, i]
                copies.append(pltpu.make_async_copy(ref.at[done], out.at[done], sem))
                copies[-1].start()
    for copy in copies:
        copy.wait()


def attention(scal, query, out_grad, key, value, halo_c, halo_x, last):
    rows, width = query.shape
    reach = halo_c.shape[1]
    keys = rows + 2 * reach
    every = next(n for n in (4, 2) if width % (n * HEAD) == 0) * HEAD
    vmem = pl.BlockSpec(memory_space=pltpu.VMEM)
    flat = jax.ShapeDtypeStruct((rows, width), BF16)
    half = jax.ShapeDtypeStruct((2, reach, width), BF16)
    return pl.pallas_call(
        functools.partial(attention_kernel, reach, last, every),
        in_specs=[pl.BlockSpec(memory_space=pltpu.SMEM)] + [vmem] * 6,
        out_specs=[pl.BlockSpec(memory_space=pltpu.HBM)] * 5,
        out_shape=[flat] * 3 + [half] * 2,
        scratch_shapes=[pltpu.VMEM(out.shape, out.dtype) for out in [flat] * 3 + [half] * 2]
        + [pltpu.SemaphoreType.DMA((width // every, 5))],
        cost_estimate=cost(
            20 * rows * keys * width, 22 * width * rows, width // HEAD * rows * keys
        ),
        compiler_params=pltpu.CompilerParams(vmem_limit_bytes=14 << 20),
        name="window_attention",
    )(scal, query, out_grad, key, value, halo_c, halo_x)


def scores_kernel(scal, k0, q0, *refs):
    twos, out = refs[:-1], refs[-1]
    even = scal[1] % 2 == 0

    def fill(arrays):
        k1, queries = arrays[0], arrays[1:]
        out[0] = dot_last(q0[...], k1[...]).astype(BF16)
        for n in range((out.shape[0] - 1) // 2):
            out[2 * n + 1] = dot_last(queries[n][...], k0[...]).astype(BF16)
            out[2 * n + 2] = dot_last(queries[n][...], k1[...]).astype(BF16)

    @pl.when(even)
    def _():
        fill(twos)

    @pl.when(jnp.logical_not(even))
    def _():
        fill([twos[n ^ 1] for n in range(len(twos))])


def scores(scal, k0, q0, twos, pairs):
    rows, width = k0.shape
    vmem = pl.BlockSpec(memory_space=pltpu.VMEM)
    return pl.pallas_call(
        scores_kernel,
        in_specs=[pl.BlockSpec(memory_space=pltpu.SMEM)] + [vmem] * (2 + len(twos)),
        out_specs=vmem,
        out_shape=jax.ShapeDtypeStruct((pairs, rows, rows), BF16),
        cost_estimate=cost(
            2 * pairs * rows * rows * width, 2 * (pairs * rows * rows + (2 + pairs) * rows * width)
        ),
        compiler_params=pltpu.CompilerParams(vmem_limit_bytes=20 << 20),
        name="pair_scores",
    )(scal, k0, q0, *twos)


def rates_kernel(share, together, f0, f1, st, g0, *refs):
    moved, out = refs[:-1], refs[-1]
    lanes = out.shape[2]
    step = st.shape[2] // 2
    for block in range(0, st.shape[2], step):
        rows = slice(block, block + step)

        def pair(n, g, f):
            products = dot_last(g[...], f[rows, :])
            summed = jnp.sum(st[n, :, rows].astype(F32) * products, axis=0, keepdims=True)
            return summed * (together[n : n + 1, 0:1] * share)

        before = pair(0, g0, f1)
        own = jnp.zeros_like(before)
        for n, g in enumerate(moved):
            own += pair(2 * n + 1, g, f0)
            before += pair(2 * n + 2, g, f1)
        for at in range(0, step, lanes):
            part = slice(at, at + lanes)
            n = (block + at) // lanes
            out[n, 0:1, :] = own[:, part]
            out[n, 1:2, :] = before[:, part]


def rates(together, f0, f1, st, g0, moved, tiles):
    rows, width = f0.shape
    pairs = st.shape[0]
    vmem = pl.BlockSpec(memory_space=pltpu.VMEM)
    return pl.pallas_call(
        functools.partial(rates_kernel, 1.0 / rows),
        in_specs=[vmem] * (5 + len(moved)),
        out_specs=vmem,
        out_shape=jax.ShapeDtypeStruct((tiles, 2, rows // tiles), F32),
        cost_estimate=cost(
            2 * pairs * rows * rows * width, 2 * (pairs * rows * rows + (2 + pairs) * rows * width)
        ),
        compiler_params=pltpu.CompilerParams(vmem_limit_bytes=16 << 20),
        name="pair_rates",
    )(together, f0, f1, st, g0, *moved)


def margins_kernel(scal, dk, dv, mc, mx, key_grad, value_grad):
    reach = mc.shape[1]
    even = scal[1] % 2 == 0
    for i, (own, out) in enumerate(((dk, key_grad), (dv, value_grad))):
        from_c, from_x = mc[i].astype(F32), mx[i].astype(F32)
        head = jnp.where(even, from_x, from_c)
        tail = jnp.where(even, from_c, from_x)
        out[:reach] = (own[:reach].astype(F32) + head).astype(BF16)
        out[reach:] = (own[reach:].astype(F32) + tail).astype(BF16)


def add_margins(scal, dk, dv, mc, mx):
    rows, width = dk.shape
    vmem = pl.BlockSpec(memory_space=pltpu.VMEM)
    return pl.pallas_call(
        margins_kernel,
        in_specs=[pl.BlockSpec(memory_space=pltpu.SMEM)] + [vmem] * 4,
        out_specs=[vmem] * 2,
        out_shape=[jax.ShapeDtypeStruct((rows, width), BF16)] * 2,
        input_output_aliases={1: 0, 2: 1},
        cost_estimate=cost(2 * rows * width, 12 * rows * width),
        compiler_params=pltpu.CompilerParams(vmem_limit_bytes=8 << 20),
        name="add_margins",
    )(scal, dk, dv, mc, mx)


def sum_kernel(parts, out):
    total = parts[0].astype(F32)
    for n in range(1, parts.shape[0]):
        total += parts[n].astype(F32)
    out[...] = total.astype(BF16)


def sum_parts(parts):
    vmem = pl.BlockSpec(memory_space=pltpu.VMEM)
    return pl.pallas_call(
        sum_kernel,
        in_specs=[vmem],
        out_specs=vmem,
        out_shape=jax.ShapeDtypeStruct(parts.shape[1:], BF16),
        cost_estimate=cost(parts.size, 2 * parts.size),
        compiler_params=pltpu.CompilerParams(vmem_limit_bytes=8 << 20),
        name="sum_parts",
    )(parts)


def shifted(array, axis, by):
    devices = lax.axis_size(axis)
    pairs = [(i + by, i) for i in range(devices) if 0 <= i + by < devices]
    return lax.ppermute(array, axis, pairs)


def swapped(array, axis, first):
    devices = lax.axis_size(axis)
    pairs = [(i, i + 1) for i in range(first, devices - 1, 2)]
    return lax.ppermute(array, axis, pairs + [(j, i) for i, j in pairs])


def moved_apart(array, by_even, by_odd):
    groups, tiles = lax.axis_size("tm"), lax.axis_size("space")
    pairs = []
    for group in range(groups):
        for tile in range(tiles):
            source = group + (by_odd if tile % 2 else by_even)
            if 0 <= source < groups:
                pairs.append((source * tiles + tile, group * tiles + tile))
    return lax.ppermute(array, ("tm", "space"), pairs)


def per_device(
    attn_query,
    attn_key,
    attn_value,
    attn_outgrad,
    fast_query,
    fast_outgrad,
    fast_key,
    gate_weights,
    up_weights,
    down_weights,
    gate_factor,
    clip_groups,
):
    groups, tiles = lax.axis_size("tm"), lax.axis_size("space")
    group, tile = lax.axis_index("tm"), lax.axis_index("space")
    scal = jnp.stack([group, tile]).astype(jnp.int32)
    rows = fast_query.shape[0]
    tile_rows, _ = attn_query.shape
    most = groups // 2
    shifts = tuple(range(2, most, 2))
    travels = [-1, *shifts]
    travels += travels[-1:] * (len(travels) % 2)

    outgoing, halo_c, halo_x = pick(scal, fast_key, fast_query, attn_key, attn_value)
    received = []
    for n in range(0, len(travels), 2):
        array = outgoing if n == 0 else fast_query
        received.append(moved_apart(array, travels[n], travels[n + 1]))
    together = pair_weights(scal, clip_groups, shifts)
    factor_before = shifted(gate_factor, "tm", -1)
    halo_c = swapped(halo_c, "space", 0)
    halo_x = swapped(halo_x, "space", 1)

    gate_grad_b, input_part = fast(fast_query, fast_outgrad, gate_weights, up_weights, down_weights)
    moved = []
    for v in shifts:
        moved.append(shifted(gate_grad_b, "tm", v))

    parts = lax.all_to_all(input_part.reshape(tiles, tile_rows, -1), "space", 0, 0)

    query_grad, dk, dv, margin_c, margin_x = attention(
        scal, attn_query, attn_outgrad, attn_key, attn_value, halo_c, halo_x, rows
    )
    margin_c = swapped(margin_c, "space", 0)
    margin_x = swapped(margin_x, "space", 1)

    twos = []
    for array in received:
        twos += [array, swapped(array, "space", 0)]
    st = scores(scal, fast_key, fast_query, twos, 1 + 2 * len(shifts))
    fast_grad = sum_parts(parts)
    key_grad, value_grad = add_margins(scal, dk, dv, margin_c, margin_x)
    rate = rates(together, gate_factor, factor_before, st, gate_grad_b, moved, tiles)
    rate = lax.all_to_all(rate, "space", 0, 0)
    rate = jnp.sum(rate, axis=0)
    rate_grad = rate[0] + shifted(rate[1], "tm", 1)
    return query_grad, key_grad, value_grad, fast_grad, rate_grad


def solution(mesh):
    over = ("tm", "space")
    tiled = P(over, None)
    in_specs = (
        (tiled,) * 4
        + (P("tm", None),) * 3
        + (P("tm", None, "space"),) * 2
        + (P("tm", "space", None), P("tm", "space"), P())
    )
    return jax.shard_map(
        per_device,
        mesh=mesh,
        in_specs=in_specs,
        out_specs=(tiled,) * 4 + (P(over),),
        check_vma=False,
    )
```

```python
import functools
import math

import jax
import jax.numpy as jnp
from jax import lax
from jax.experimental import pallas as pl
from jax.experimental.pallas import tpu as pltpu
from jax.sharding import PartitionSpec as P


HEAD = 128

CONTRACT_LAST = (((1,), (1,)), ((), ()))
CONTRACT_FIRST = (((0,), (0,)), ((), ()))
F32 = jnp.float32
BF16 = jnp.bfloat16


def dot_last(a, b):
    return lax.dot_general(a, b, CONTRACT_LAST, preferred_element_type=F32)


def far(*arrays):
    return [pltpu.with_memory_space_constraint(array, pltpu.HBM) for array in arrays]


def near(*arrays):
    return [pltpu.with_memory_space_constraint(array, pltpu.VMEM) for array in arrays]


def room(least, needed):
    return pltpu.CompilerParams(vmem_limit_bytes=max(least << 20, needed))


def cost(flops, moved, transcendentals=0):
    return pl.CostEstimate(flops=flops, bytes_accessed=moved, transcendentals=transcendentals)


def pick_kernel(scal, fk, fq, out, sem):
    odd = scal[0] % 2
    copy = pltpu.make_async_copy(fk, out, sem)
    pl.when(odd == 0)(copy.start)
    pl.when(odd == 1)(pltpu.make_async_copy(fq, out, sem).start)
    copy.wait()


def pick(scal, fast_key, fast_query):
    return pl.pallas_call(
        pick_kernel,
        in_specs=[pl.BlockSpec(memory_space=pltpu.SMEM)]
        + [pl.BlockSpec(memory_space=pltpu.HBM)] * 2,
        out_specs=pl.BlockSpec(memory_space=pltpu.VMEM),
        out_shape=pltpu.VMEM(fast_key.shape, BF16),
        scratch_shapes=[pltpu.SemaphoreType.DMA],
        cost_estimate=cost(0, 4 * fast_key.size),
        compiler_params=pltpu.CompilerParams(vmem_limit_bytes=4 << 20),
        name="pick_outgoing",
    )(scal, *far(fast_key, fast_query))


def halos_kernel(scal, k, v, hc, hx, sems):
    reach = hc.shape[1]
    odd = scal[0] % 2
    copies = []
    for i, source in enumerate((k, v)):
        for j, (half, at) in enumerate(((hx, odd), (hc, 1 - odd))):
            rows = pl.ds(pl.multiple_of(at * reach, reach), reach)
            copies.append(pltpu.make_async_copy(source.at[rows], half.at[i], sems.at[i, j]))
    for copy in copies:
        copy.start()
    for copy in copies:
        copy.wait()


def pick_halos(scal, key, value):
    rows, width = key.shape
    half = jax.ShapeDtypeStruct((2, rows // 2, width), BF16)
    return pl.pallas_call(
        halos_kernel,
        in_specs=[pl.BlockSpec(memory_space=pltpu.SMEM)]
        + [pl.BlockSpec(memory_space=pltpu.HBM)] * 2,
        out_specs=[pl.BlockSpec(memory_space=pltpu.VMEM)] * 2,
        out_shape=[half, half],
        scratch_shapes=[pltpu.SemaphoreType.DMA((2, 2))],
        cost_estimate=cost(0, 8 * rows * width),
        compiler_params=pltpu.CompilerParams(vmem_limit_bytes=4 << 20),
        name="pick_halos",
    )(scal, *far(key, value))


def weights_kernel(shifts, tiles, scal, clips, out):
    at = lax.div(scal[0], tiles)
    starts, total = [], 0
    for n in range(clips.shape[0]):
        starts.append(total)
        total = total + clips[n]

    def together(u, v):
        apart = jnp.bool_(False)
        for x in range(1 - u, v + 1):
            for start in starts:
                apart = apart | (start == at + x)
        return jnp.where(apart, 0.0, 1.0)

    for n, (u, v) in enumerate([(1, 0)] + [(u, v) for v in shifts for u in (0, 1)]):
        out[n : n + 1, :] = jnp.full((1, out.shape[1]), together(u, v), F32)


def pair_weights(scal, clips, shifts, tiles):
    return pl.pallas_call(
        functools.partial(weights_kernel, shifts, tiles),
        in_specs=[pl.BlockSpec(memory_space=pltpu.SMEM)] * 2,
        out_specs=pl.BlockSpec(memory_space=pltpu.VMEM),
        out_shape=jax.ShapeDtypeStruct((1 + 2 * len(shifts), HEAD), F32),
        cost_estimate=cost(20 * 10**9, 4096),
        compiler_params=pltpu.CompilerParams(vmem_limit_bytes=1 << 20),
        name="pair_weights",
    )(scal, clips)


def fast_kernel(step, q, og, gw, uw, dw, gate_out, part_out, gate_grad, up_grad, part, sems):
    for j in range(gw.shape[2] // step):
        cols = slice(j * step, (j + 1) * step)
        gate = jnp.dot(q[...], gw[0, :, cols], preferred_element_type=F32)
        up = jnp.dot(q[...], uw[0, :, cols], preferred_element_type=F32)
        hidden = dot_last(og[...], dw[0, cols, :])
        sig = jax.nn.sigmoid(gate)
        gate_grad[:, cols] = (hidden * up * sig * (1.0 + gate * (1.0 - sig))).astype(BF16)
        up_grad[:, cols] = (hidden * (gate * sig)).astype(BF16)
    copies = [pltpu.make_async_copy(gate_grad, gate_out, sems.at[0])]
    copies[0].start()
    for j in range(q.shape[1] // step):
        rows = slice(j * step, (j + 1) * step)
        part[:, rows] = (
            dot_last(gate_grad[...], gw[0, rows, :]) + dot_last(up_grad[...], uw[0, rows, :])
        ).astype(BF16)
        copy = pltpu.make_async_copy(part.at[:, rows], part_out.at[:, rows], sems.at[1 + j])
        copy.start()
        copies.append(copy)
    for copy in copies:
        copy.wait()


def fast(query, outgrad, gate_w, up_w, down_w):
    rows, width = query.shape
    hidden = gate_w.shape[2]
    step = next(s for s in (256, 128) if hidden % s == 0 and width % s == 0)
    vmem = pl.BlockSpec(memory_space=pltpu.VMEM)
    return pl.pallas_call(
        functools.partial(fast_kernel, step),
        in_specs=[vmem] * 5,
        out_specs=[pl.BlockSpec(memory_space=pltpu.HBM)] * 2,
        out_shape=[pltpu.HBM((rows, n), BF16) for n in (hidden, width)],
        scratch_shapes=[
            pltpu.VMEM((rows, hidden), BF16),
            pltpu.VMEM((rows, hidden), BF16),
            pltpu.VMEM((rows, width), BF16),
            pltpu.SemaphoreType.DMA((1 + width // step,)),
        ],
        cost_estimate=cost(20 * 10**9, 6 * width * hidden + 8 * rows * width),
        compiler_params=room(16, (6 * rows * width + 6 * width * hidden + 4 * rows * hidden) * 5 // 4),
        name="fast_weights",
    )(query, outgrad, gate_w, up_w, down_w)


def bias_kernel(reach, last, scal, out):
    keys, rows = out.shape[0], out.shape[1] // 2
    at = lax.rem(scal[0], last // rows)
    even = at % 2 == 0
    key_row = lax.broadcasted_iota(jnp.int32, (keys, rows), 0)
    query_row = lax.broadcasted_iota(jnp.int32, (keys, rows), 1)
    shift_c = jnp.where(even, 0, -(rows + reach))
    shift_x = jnp.where(even, -(rows + 2 * reach), -reach)
    key_pos = key_row + jnp.where(
        key_row < rows, 0, jnp.where(key_row < rows + reach, shift_c, shift_x)
    )
    offset = at * rows
    live = (key_pos + offset >= 0) & (key_pos + offset < last)
    bias = jnp.where(live & (jnp.abs(key_pos - query_row) <= reach), 0.0, -1e30)
    out[:, :rows] = bias
    out[:, rows:] = bias


def window_bias(scal, rows, reach, last):
    return pl.pallas_call(
        functools.partial(bias_kernel, reach, last),
        in_specs=[pl.BlockSpec(memory_space=pltpu.SMEM)],
        out_specs=pl.BlockSpec(memory_space=pltpu.VMEM),
        out_shape=jax.ShapeDtypeStruct((rows + 2 * reach, 2 * rows), F32),
        cost_estimate=cost(20 * 10**9, 16 * rows * rows),
        compiler_params=pltpu.CompilerParams(vmem_limit_bytes=2 << 20),
        name="window_bias",
    )(scal)


def attention_kernel(every, bias, *refs):
    sources, outs, local, held = refs[:6], refs[6:11], refs[11:17], refs[17:22]
    load_sems, sems = refs[22:]
    q, g, k, v, hc, hx = local
    dk_own, dv_own, dq, mc, mx = held
    loads, copies = [], []
    for at in range(0, q.shape[1], every):
        part = (Ellipsis, slice(at, at + every))
        for i, (source, ref) in enumerate(zip(sources, local)):
            sem = load_sems.at[at // every, i]
            loads.append(pltpu.make_async_copy(source.at[part], ref.at[part], sem))
            loads[-1].start()
    rows, reach = q.shape[0], hc.shape[1]
    wide = 2 * HEAD
    scaling = 1.0 / math.sqrt(HEAD)
    zero = jnp.zeros((rows, HEAD), BF16)

    def diagonal(ref, at):
        head, other = ref[:, at : at + HEAD], ref[:, at + HEAD : at + wide]
        return jnp.concatenate(
            [jnp.concatenate([head, zero], axis=1), jnp.concatenate([zero, other], axis=1)], axis=0
        )

    for start in range(0, q.shape[1], wide):
        if start % every == 0:
            for copy in loads[start // every * 6 : start // every * 6 + 6]:
                copy.wait()
        col = slice(start, start + wide)
        kk = jnp.concatenate([k[:, col], hc[0, :, col], hx[0, :, col]], axis=0)
        vv = jnp.concatenate([v[:, col], hc[1, :, col], hx[1, :, col]], axis=0)
        qd, gd = diagonal(q, start), diagonal(g, start)
        scores = dot_last(kk, qd) * scaling + bias[...]
        exponent = jnp.exp(scores - jnp.max(scores, axis=0, keepdims=True))
        probs = exponent * (1.0 / jnp.sum(exponent, axis=0, keepdims=True))
        probs_b = probs.astype(BF16)
        dprobs = dot_last(vv, gd)
        delta = jnp.sum(probs_b.astype(F32) * dprobs, axis=0, keepdims=True)
        dscores_b = (probs * (dprobs - delta)).astype(BF16)
        dv = jnp.dot(probs_b, gd, preferred_element_type=F32)
        dk = jnp.dot(dscores_b, qd, preferred_element_type=F32) * scaling
        both = lax.dot_general(dscores_b, kk, CONTRACT_FIRST, preferred_element_type=F32)
        dq[:, start : start + HEAD] = (both[:rows, :HEAD] * scaling).astype(BF16)
        dq[:, start + HEAD : start + wide] = (both[rows:, HEAD:] * scaling).astype(BF16)
        for i, (grad, own) in enumerate(((dk, dk_own), (dv, dv_own))):
            own[:, col] = grad[:rows].astype(BF16)
            mc[i, :, col] = grad[rows : rows + reach].astype(BF16)
            mx[i, :, col] = grad[rows + reach :].astype(BF16)
        if (start + wide) % every == 0:
            done = (Ellipsis, slice(start + wide - every, start + wide))
            for i, (ref, out) in enumerate(zip(held, outs)):
                sem = sems.at[start // every, i]
                copies.append(pltpu.make_async_copy(ref.at[done], out.at[done], sem))
                copies[-1].start()
    for copy in copies:
        copy.wait()


def attention(bias, query, out_grad, key, value, halo_c, halo_x):
    rows, width = query.shape
    reach = halo_c.shape[1]
    keys = rows + 2 * reach
    every = next(n for n in (10, 4, 2) if width % (n * HEAD) == 0) * HEAD
    vmem = pl.BlockSpec(memory_space=pltpu.VMEM)
    flat, half = (rows, width), (2, reach, width)
    return pl.pallas_call(
        functools.partial(attention_kernel, every),
        in_specs=[vmem] + [pl.BlockSpec(memory_space=pltpu.HBM)] * 6,
        out_specs=[pl.BlockSpec(memory_space=pltpu.HBM)] * 5,
        out_shape=[pltpu.HBM(x, BF16) for x in (flat, flat, flat, half, half)],
        scratch_shapes=[pltpu.VMEM(x, BF16) for x in [flat] * 4 + [half] * 2 + [flat] * 3 + [half] * 2]
        + [pltpu.SemaphoreType.DMA((width // every, 6)), pltpu.SemaphoreType.DMA((width // every, 5))],
        cost_estimate=cost(
            20 * rows * keys * width, 22 * width * rows, width // HEAD * rows * keys
        ),
        compiler_params=pltpu.CompilerParams(vmem_limit_bytes=14 << 20),
        name="window_attention",
    )(bias, *far(query, out_grad, key, value, halo_c, halo_x))


def scores_kernel(n_two, scal, k0, q0, *refs):
    paired, received, out = refs[:n_two], refs[n_two : 2 * n_two], refs[2 * n_two]
    local, held, load_sems, sems = refs[2 * n_two + 1 : 3 * n_two + 1], *refs[3 * n_two + 1 :]
    odd = scal[0] % 2
    loads = [
        pltpu.make_async_copy(source, ref, load_sems.at[n])
        for n, (source, ref) in enumerate(zip(received, local))
    ]
    for copy in loads:
        copy.start()

    def work(side):
        arrays = []
        for n in range(n_two):
            both = [(local[n], loads[n]), (paired[n], None)]
            arrays += both[::-1] if side else both
        k1, queries = arrays[0], arrays[1:]
        pairs = [(0, (q0, None), k1)]
        for n in range((held.shape[0] - 1) // 2):
            pairs += [(2 * n + 1, queries[n], (k0, None)), (2 * n + 2, queries[n], k1)]
        pairs.sort(key=lambda pair: sum(load is not None for _, load in pair[1:]))
        copies, waited = [], []
        for n, (q, load_q), (k, load_k) in pairs:
            for load in (load_q, load_k):
                if load is not None and id(load) not in waited:
                    load.wait()
                    waited.append(id(load))
            held[n] = dot_last(q[...], k[...]).astype(BF16)
            copies.append(pltpu.make_async_copy(held.at[n], out.at[n], sems.at[n]))
            copies[-1].start()
        for copy in [load for load in loads if id(load) not in waited] + copies:
            copy.wait()

    pl.when(odd == 0)(functools.partial(work, 0))
    pl.when(odd == 1)(functools.partial(work, 1))


def scores(scal, k0, q0, received, paired, pairs):
    rows, width = k0.shape
    n_two = len(received)
    vmem = pl.BlockSpec(memory_space=pltpu.VMEM)
    hbm = pl.BlockSpec(memory_space=pltpu.HBM)
    return pl.pallas_call(
        functools.partial(scores_kernel, n_two),
        in_specs=[pl.BlockSpec(memory_space=pltpu.SMEM)] + [vmem] * (2 + n_two) + [hbm] * n_two,
        out_specs=hbm,
        out_shape=pltpu.HBM((pairs, rows, rows), BF16),
        scratch_shapes=[pltpu.VMEM((rows, width), BF16)] * n_two
        + [
            pltpu.VMEM((pairs, rows, rows), BF16),
            pltpu.SemaphoreType.DMA((n_two,)),
            pltpu.SemaphoreType.DMA((pairs,)),
        ],
        cost_estimate=cost(20 * 10**9, 2 * pairs * rows * rows),
        compiler_params=room(20, 14 * pairs * rows * rows // 3 + 4 * (1 + n_two) * rows * width),
        name="pair_scores",
    )(scal, k0, q0, *paired, *far(*received))


def rates_kernel(share, n_far, scal, together, st, g0, *refs):
    sources, own_out, before_out = refs[:n_far], refs[n_far], refs[n_far + 1]
    held, sems = refs[n_far + 2 : -1], refs[-1]
    f1, moved, f0 = held[0], held[1:-1], held[-1]
    loads = [
        pltpu.make_async_copy(source, ref, sems.at[n])
        for n, (source, ref) in enumerate(zip(sources, held))
    ]
    for copy in loads:
        copy.start()
    lanes = own_out.shape[2]

    def pair(n, g, f):
        products = dot_last(g[...], f[...])
        summed = jnp.sum(st[n].astype(F32) * products, axis=0, keepdims=True)
        return summed * (together[n : n + 1, 0:1] * share)

    loads[0].wait()
    before = pair(0, g0, f1)
    own = jnp.zeros_like(before)
    for n, g in enumerate(moved):
        loads[1 + n].wait()
        before += pair(2 * n + 2, g, f1)
    loads[-1].wait()
    for n, g in enumerate(moved):
        own += pair(2 * n + 1, g, f0)
    for n in range(own_out.shape[0]):
        part = slice(n * lanes, (n + 1) * lanes)
        own_out[n] = own[:, part]
        before_out[n] = before[:, part]


def rates(scal, together, st, f0, f1, g0, moved, tiles):
    rows, width = f0.shape
    pairs = st.shape[0]
    vmem = pl.BlockSpec(memory_space=pltpu.VMEM)
    n_far = 2 + len(moved)
    return pl.pallas_call(
        functools.partial(rates_kernel, 1.0 / rows, n_far),
        in_specs=[pl.BlockSpec(memory_space=pltpu.SMEM)]
        + [vmem] * 3
        + [pl.BlockSpec(memory_space=pltpu.HBM)] * n_far,
        out_specs=[vmem] * 2,
        out_shape=[jax.ShapeDtypeStruct((tiles, 1, rows // tiles), F32)] * 2,
        scratch_shapes=[pltpu.VMEM((rows, width), BF16)] * n_far
        + [pltpu.SemaphoreType.DMA((n_far,))],
        cost_estimate=cost(
            2 * pairs * rows * rows * width, 2 * (pairs * rows * rows + (2 + pairs) * rows * width)
        ),
        compiler_params=room(14, (2 * pairs + 16) * rows * rows + 4 * (1 + n_far) * rows * width),
        name="pair_rates",
    )(scal, *near(together, st, g0), *far(f1, *moved, f0))


def fold_kernel(bit, scal, kept, received, *outs):
    if len(outs) == 1:
        outs[0][...] = kept[...] + received[...]
        return
    keep, send = outs
    side = lax.rem(lax.div(scal[0], 1 << bit), 2)
    for n in range(kept.shape[0]):
        total = kept[n] + received[n]

        def put(ref):
            ref[n // 2] = total

        pl.when(side == n % 2)(functools.partial(put, keep))
        pl.when(side != n % 2)(functools.partial(put, send))


def fold(scal, kept, received, bit):
    vmem = pl.BlockSpec(memory_space=pltpu.VMEM)
    last = kept.shape[0] == 1
    shape = kept.shape if last else (kept.shape[0] // 2, *kept.shape[1:])
    out = jax.ShapeDtypeStruct(shape, kept.dtype)
    return pl.pallas_call(
        functools.partial(fold_kernel, bit),
        in_specs=[pl.BlockSpec(memory_space=pltpu.SMEM), vmem, vmem],
        out_specs=[vmem] if last else [vmem] * 2,
        out_shape=[out] if last else [out] * 2,
        cost_estimate=cost(kept.size, 12 * kept.size),
        compiler_params=pltpu.CompilerParams(vmem_limit_bytes=1 << 20),
        name="fold_rates",
    )(scal, kept, received)


def margins_kernel(parts, scal, dk, dv, mc, mx, *refs):
    outs, (own, core, chip, done), (load_sems, sems) = refs[:2], refs[2:6], refs[6:]
    even = scal[0] % 2 == 0
    reach = mc.shape[1]
    step = dk.shape[1] // parts
    steps = [(i, slice(n * step, (n + 1) * step)) for i in range(2) for n in range(parts)]
    loads, copies = [], []
    for n, (i, cols) in enumerate(steps):
        moves = (
            ((dk, dv)[i].at[:, cols], own.at[i, :, cols]),
            (mc.at[i, :, cols], core.at[i, :, cols]),
            (mx.at[i, :, cols], chip.at[i, :, cols]),
        )
        loads.append([pltpu.make_async_copy(*move, load_sems.at[n, j]) for j, move in enumerate(moves)])
        for copy in loads[-1]:
            copy.start()
    for n, (i, cols) in enumerate(steps):
        for copy in loads[n]:
            copy.wait()
        from_c, from_x = core[i, :, cols].astype(F32), chip[i, :, cols].astype(F32)
        head = jnp.where(even, from_x, from_c)
        tail = jnp.where(even, from_c, from_x)
        done[i, :reach, cols] = (own[i, :reach, cols].astype(F32) + head).astype(BF16)
        done[i, reach:, cols] = (own[i, reach:, cols].astype(F32) + tail).astype(BF16)
        copies.append(pltpu.make_async_copy(done.at[i, :, cols], outs[i].at[:, cols], sems.at[n]))
        copies[-1].start()
    for copy in copies:
        copy.wait()


def add_margins(scal, dk, dv, mc, mx):
    rows, width = dk.shape
    parts = next(n for n in (2, 1) if width % (n * HEAD) == 0)
    hbm = pl.BlockSpec(memory_space=pltpu.HBM)
    whole, half = (2, rows, width), (2, rows // 2, width)
    return pl.pallas_call(
        functools.partial(margins_kernel, parts),
        in_specs=[pl.BlockSpec(memory_space=pltpu.SMEM)]
        + [hbm] * 2
        + [pl.BlockSpec(memory_space=pl.ANY)] * 2,
        out_specs=[hbm] * 2,
        out_shape=[pltpu.HBM((rows, width), BF16)] * 2,
        scratch_shapes=[pltpu.VMEM(x, BF16) for x in (whole, half, half, whole)]
        + [pltpu.SemaphoreType.DMA((2 * parts, 3)), pltpu.SemaphoreType.DMA((2 * parts,))],
        cost_estimate=cost(2 * rows * width, 12 * rows * width),
        compiler_params=pltpu.CompilerParams(vmem_limit_bytes=8 << 20),
        name="add_margins",
    )(scal, *far(dk, dv), mc, mx)


def sum_kernel(parts, out):
    total = parts[0].astype(F32)
    for n in range(1, parts.shape[0]):
        total += parts[n].astype(F32)
    out[...] = total.astype(BF16)


def sum_parts(parts):
    vmem = pl.BlockSpec(memory_space=pltpu.VMEM)
    return pl.pallas_call(
        sum_kernel,
        in_specs=[vmem],
        out_specs=vmem,
        out_shape=jax.ShapeDtypeStruct(parts.shape[1:], BF16),
        cost_estimate=cost(parts.size, 2 * parts.size),
        compiler_params=pltpu.CompilerParams(vmem_limit_bytes=8 << 20),
        name="sum_parts",
    )(parts)


def shifted(array, axis, by):
    devices = lax.axis_size(axis)
    pairs = [(i + by, i) for i in range(devices) if 0 <= i + by < devices]
    return lax.ppermute(array, axis, pairs)


def swapped(array, axis, first):
    devices = lax.axis_size(axis)
    pairs = [(i, i + 1) for i in range(first, devices - 1, 2)]
    return lax.ppermute(array, axis, pairs + [(j, i) for i, j in pairs])


def across(array, axis, bit):
    pairs = [(i, i ^ (1 << bit)) for i in range(lax.axis_size(axis))]
    return lax.ppermute(array, axis, pairs)


def moved_apart(array, by_even, by_odd):
    groups, tiles = lax.axis_size("tm"), lax.axis_size("space")
    pairs = []
    for group in range(groups):
        for tile in range(tiles):
            source = group + (by_odd if tile % 2 else by_even)
            if 0 <= source < groups:
                pairs.append((source * tiles + tile, group * tiles + tile))
    return lax.ppermute(array, ("tm", "space"), pairs)


def per_device(
    attn_query,
    attn_key,
    attn_value,
    attn_outgrad,
    fast_query,
    fast_outgrad,
    fast_key,
    gate_weights,
    up_weights,
    down_weights,
    gate_factor,
    clip_groups,
):
    groups, tiles = lax.axis_size("tm"), lax.axis_size("space")
    scal = lax.axis_index(("tm", "space")).astype(jnp.int32).reshape(1)
    rows = fast_query.shape[0]
    tile_rows, _ = attn_query.shape
    most = groups // 2
    shifts = tuple(range(2, most, 2))
    travels = [-1, *shifts]
    travels += travels[-1:] * (len(travels) % 2)

    outgoing = pick(scal, fast_key, fast_query)
    received = []
    for n in range(0, len(travels), 2):
        array = outgoing if n == 0 else fast_query
        received.append(moved_apart(array, travels[n], travels[n + 1]))
    together = pair_weights(scal, clip_groups, shifts, tiles)
    factor_before = shifted(gate_factor, "tm", -1)
    halo_c, halo_x = pick_halos(scal, attn_key, attn_value)
    halo_c = swapped(halo_c, "space", 0)
    halo_x = swapped(halo_x, "space", 1)

    gate_grad_b, input_part = fast(fast_query, fast_outgrad, gate_weights, up_weights, down_weights)
    moved = []
    for v in shifts:
        moved.append(shifted(gate_grad_b, "tm", v))

    parts = lax.all_to_all(input_part.reshape(tiles, tile_rows, -1), "space", 0, 0)

    bias = window_bias(scal, tile_rows, tile_rows // 2, rows)
    dk, dv, query_grad, margin_c, margin_x = attention(
        bias, attn_query, attn_outgrad, attn_key, attn_value, halo_c, halo_x
    )
    margin_c = swapped(margin_c, "space", 0)
    margin_x = swapped(margin_x, "space", 1)

    paired = []
    for array in received:
        paired.append(swapped(array, "space", 0))
    pairs = 1 + 2 * len(shifts)
    st = scores(scal, fast_key, fast_query, received, paired, pairs)
    fast_grad = sum_parts(parts)
    own, before = rates(scal, together, st, gate_factor, factor_before, gate_grad_b, moved, tiles)
    arrived = shifted(before, "tm", 1)
    key_grad, value_grad = add_margins(scal, dk, dv, margin_c, margin_x)
    kept = own
    for bit in range(tiles.bit_length()):
        kept, *rest = fold(scal, kept, arrived, bit)
        if rest:
            arrived = across(rest[0], "space", bit)
    rate_grad = kept.reshape(-1)
    return query_grad, key_grad, value_grad, fast_grad, rate_grad


def solution(mesh):
    over = ("tm", "space")
    tiled = P(over, None)
    in_specs = (
        (tiled,) * 4
        + (P("tm", None),) * 3
        + (P("tm", None, "space"),) * 2
        + (P("tm", "space", None), P("tm", "space"), P())
    )
    return jax.shard_map(
        per_device,
        mesh=mesh,
        in_specs=in_specs,
        out_specs=(tiled,) * 4 + (P(over),),
        check_vma=False,
    )
```

```python
import functools
import math

import jax
import jax.numpy as jnp
from jax import lax
from jax.experimental import pallas as pl
from jax.experimental.pallas import tpu as pltpu
from jax.sharding import PartitionSpec as P


HEAD = 128

CONTRACT_LAST = (((1,), (1,)), ((), ()))
CONTRACT_FIRST = (((0,), (0,)), ((), ()))
F32 = jnp.float32
BF16 = jnp.bfloat16


def dot_last(a, b):
    return lax.dot_general(a, b, CONTRACT_LAST, preferred_element_type=F32)


def far(*arrays):
    return [pltpu.with_memory_space_constraint(array, pltpu.HBM) for array in arrays]


def near(*arrays):
    return [pltpu.with_memory_space_constraint(array, pltpu.VMEM) for array in arrays]


def room(least, needed):
    return pltpu.CompilerParams(vmem_limit_bytes=max(least << 20, needed))


def cost(flops, moved, transcendentals=0):
    return pl.CostEstimate(flops=flops, bytes_accessed=moved, transcendentals=transcendentals)


def pick_kernel(scal, fk, fq, out, sem):
    odd = scal[0] % 2
    copy = pltpu.make_async_copy(fk, out, sem)
    pl.when(odd == 0)(copy.start)
    pl.when(odd == 1)(pltpu.make_async_copy(fq, out, sem).start)
    copy.wait()


def pick(scal, fast_key, fast_query):
    return pl.pallas_call(
        pick_kernel,
        in_specs=[pl.BlockSpec(memory_space=pltpu.SMEM)]
        + [pl.BlockSpec(memory_space=pltpu.HBM)] * 2,
        out_specs=pl.BlockSpec(memory_space=pltpu.VMEM),
        out_shape=pltpu.VMEM(fast_key.shape, BF16),
        scratch_shapes=[pltpu.SemaphoreType.DMA],
        cost_estimate=cost(0, 4 * fast_key.size),
        compiler_params=pltpu.CompilerParams(vmem_limit_bytes=4 << 20),
        name="pick_outgoing",
    )(scal, *far(fast_key, fast_query))


def halos_kernel(scal, k, v, hc, hx, sems):
    reach = hc.shape[1]
    odd = scal[0] % 2
    copies = []
    for i, source in enumerate((k, v)):
        for j, (half, at) in enumerate(((hx, odd), (hc, 1 - odd))):
            rows = pl.ds(pl.multiple_of(at * reach, reach), reach)
            copies.append(pltpu.make_async_copy(source.at[rows], half.at[i], sems.at[i, j]))
    for copy in copies:
        copy.start()
    for copy in copies:
        copy.wait()


def pick_halos(scal, key, value):
    rows, width = key.shape
    half = jax.ShapeDtypeStruct((2, rows // 2, width), BF16)
    return pl.pallas_call(
        halos_kernel,
        in_specs=[pl.BlockSpec(memory_space=pltpu.SMEM)]
        + [pl.BlockSpec(memory_space=pltpu.HBM)] * 2,
        out_specs=[pl.BlockSpec(memory_space=pltpu.VMEM)] * 2,
        out_shape=[half, half],
        scratch_shapes=[pltpu.SemaphoreType.DMA((2, 2))],
        cost_estimate=cost(0, 8 * rows * width),
        compiler_params=pltpu.CompilerParams(vmem_limit_bytes=4 << 20),
        name="pick_halos",
    )(scal, *far(key, value))


def weights_kernel(shifts, tiles, scal, clips, out):
    at = lax.div(scal[0], tiles)
    starts, total = [], 0
    for n in range(clips.shape[0]):
        starts.append(total)
        total = total + clips[n]

    def together(u, v):
        apart = jnp.bool_(False)
        for x in range(1 - u, v + 1):
            for start in starts:
                apart = apart | (start == at + x)
        return jnp.where(apart, 0.0, 1.0)

    for n, (u, v) in enumerate([(1, 0)] + [(u, v) for v in shifts for u in (0, 1)]):
        out[n : n + 1, :] = jnp.full((1, out.shape[1]), together(u, v), F32)


def pair_weights(scal, clips, shifts, tiles):
    return pl.pallas_call(
        functools.partial(weights_kernel, shifts, tiles),
        in_specs=[pl.BlockSpec(memory_space=pltpu.SMEM)] * 2,
        out_specs=pl.BlockSpec(memory_space=pltpu.VMEM),
        out_shape=jax.ShapeDtypeStruct((1 + 2 * len(shifts), HEAD), F32),
        cost_estimate=cost(20 * 10**9, 4096),
        compiler_params=pltpu.CompilerParams(vmem_limit_bytes=1 << 20),
        name="pair_weights",
    )(scal, clips)


def fast_kernel(step, ends, scal, q, og, gw, uw, dw, gate_out, keep, send, *refs):
    gate_grad, up_grad, part, gate_sem, sems = refs
    rows = keep.shape[1]
    odd = scal[0] % 2
    for j in range(gw.shape[2] // step):
        cols = slice(j * step, (j + 1) * step)
        gate = jnp.dot(q[...], gw[0, :, cols], preferred_element_type=F32)
        up = jnp.dot(q[...], uw[0, :, cols], preferred_element_type=F32)
        hidden = dot_last(og[...], dw[0, cols, :])
        sig = jax.nn.sigmoid(gate)
        gate_grad[:, cols] = (hidden * up * sig * (1.0 + gate * (1.0 - sig))).astype(BF16)
        up_grad[:, cols] = (hidden * (gate * sig)).astype(BF16)
    copies = [pltpu.make_async_copy(gate_grad, gate_out, gate_sem)]
    copies[0].start()
    begin = 0
    for at in range(0, q.shape[1], step):
        cols = slice(at, at + step)
        part[:, cols] = (
            dot_last(gate_grad[...], gw[0, cols, :]) + dot_last(up_grad[...], uw[0, cols, :])
        ).astype(BF16)
        if at + step in ends:
            cols = slice(begin, at + step)
            for n in range(2 * keep.shape[0]):
                source, sem = part.at[n * rows : (n + 1) * rows, cols], sems.at[ends.index(at + step), n]
                stay = pltpu.make_async_copy(source, keep.at[n // 2, :, cols], sem)
                leave = pltpu.make_async_copy(source, send.at[n // 2, :, cols], sem)
                pl.when(odd == n % 2)(stay.start)
                pl.when(odd != n % 2)(leave.start)
                copies.append(stay)
            begin = at + step
    for copy in copies:
        copy.wait()


def fast(scal, query, outgrad, gate_w, up_w, down_w, tiles):
    rows, width = query.shape
    hidden = gate_w.shape[2]
    step = next(s for s in (256, 128) if hidden % s == 0 and width % s == 0)
    ends = sorted({width // step * 2 // 3 * step, width})
    vmem = pl.BlockSpec(memory_space=pltpu.VMEM)
    half = pltpu.HBM((tiles // 2, rows // tiles, width), BF16)
    return pl.pallas_call(
        functools.partial(fast_kernel, step, ends),
        in_specs=[pl.BlockSpec(memory_space=pltpu.SMEM)] + [vmem] * 5,
        out_specs=[pl.BlockSpec(memory_space=pltpu.HBM)] * 3,
        out_shape=[pltpu.HBM((rows, hidden), BF16), half, half],
        scratch_shapes=[
            pltpu.VMEM((rows, hidden), BF16),
            pltpu.VMEM((rows, hidden), BF16),
            pltpu.VMEM((rows, width), BF16),
            pltpu.SemaphoreType.DMA,
            pltpu.SemaphoreType.DMA((len(ends), tiles)),
        ],
        cost_estimate=cost(20 * 10**9, 6 * width * hidden + 8 * rows * width),
        compiler_params=room(16, (6 * rows * width + 6 * width * hidden + 4 * rows * hidden) * 5 // 4),
        name="fast_weights",
    )(scal, query, outgrad, gate_w, up_w, down_w)


def bias_kernel(reach, last, scal, out):
    keys, rows = out.shape[0], out.shape[1] // 2
    at = lax.rem(scal[0], last // rows)
    even = at % 2 == 0
    key_row = lax.broadcasted_iota(jnp.int32, (keys, rows), 0)
    query_row = lax.broadcasted_iota(jnp.int32, (keys, rows), 1)
    shift_c = jnp.where(even, 0, -(rows + reach))
    shift_x = jnp.where(even, -(rows + 2 * reach), -reach)
    key_pos = key_row + jnp.where(
        key_row < rows, 0, jnp.where(key_row < rows + reach, shift_c, shift_x)
    )
    offset = at * rows
    live = (key_pos + offset >= 0) & (key_pos + offset < last)
    bias = jnp.where(live & (jnp.abs(key_pos - query_row) <= reach), 0.0, -1e30)
    out[:, :rows] = bias
    out[:, rows:] = bias


def share_kernel(share, together, out):
    out[...] = together[...] * share


def pair_shares(together, share):
    vmem = pl.BlockSpec(memory_space=pltpu.VMEM)
    return pl.pallas_call(
        functools.partial(share_kernel, share),
        in_specs=[vmem],
        out_specs=vmem,
        out_shape=jax.ShapeDtypeStruct(together.shape, F32),
        cost_estimate=cost(20 * 10**9, 4096),
        compiler_params=pltpu.CompilerParams(vmem_limit_bytes=1 << 20),
        name="pair_shares",
    )(together)


def window_bias(scal, rows, reach, last):
    return pl.pallas_call(
        functools.partial(bias_kernel, reach, last),
        in_specs=[pl.BlockSpec(memory_space=pltpu.SMEM)],
        out_specs=pl.BlockSpec(memory_space=pltpu.VMEM),
        out_shape=jax.ShapeDtypeStruct((rows + 2 * reach, 2 * rows), F32),
        cost_estimate=cost(20 * 10**9, 16 * rows * rows),
        compiler_params=pltpu.CompilerParams(vmem_limit_bytes=2 << 20),
        name="window_bias",
    )(scal)


def attention_kernel(load_ends, store_ends, bias, *refs):
    sources, outs, local, held = refs[:6], refs[6:11], refs[11:17], refs[17:22]
    load_sems, sems = refs[22:]
    q, g, k, v, hc, hx = local
    dk_own, dv_own, dq, mc, mx = held
    loads, copies = {}, []
    begin = 0
    for n, end in enumerate(load_ends):
        part = (Ellipsis, slice(begin, end))
        loads[begin] = [
            pltpu.make_async_copy(source.at[part], ref.at[part], load_sems.at[n, i])
            for i, (source, ref) in enumerate(zip(sources, local))
        ]
        for copy in loads[begin]:
            copy.start()
        begin = end
    begin, stores = 0, 0
    rows, reach = q.shape[0], hc.shape[1]
    wide = 2 * HEAD
    scaling = 1.0 / math.sqrt(HEAD)
    zero = jnp.zeros((rows, HEAD), BF16)

    def diagonal(ref, at):
        head, other = ref[:, at : at + HEAD], ref[:, at + HEAD : at + wide]
        return jnp.concatenate(
            [jnp.concatenate([head, zero], axis=1), jnp.concatenate([zero, other], axis=1)], axis=0
        )

    for start in range(0, q.shape[1], wide):
        for copy in loads.get(start, ()):
            copy.wait()
        col = slice(start, start + wide)
        kk = jnp.concatenate([k[:, col], hc[0, :, col], hx[0, :, col]], axis=0)
        vv = jnp.concatenate([v[:, col], hc[1, :, col], hx[1, :, col]], axis=0)
        qd, gd = diagonal(q, start), diagonal(g, start)
        scores = dot_last(kk, qd) * scaling + bias[...]
        exponent = jnp.exp(scores - jnp.max(scores, axis=0, keepdims=True))
        probs = exponent * (1.0 / jnp.sum(exponent, axis=0, keepdims=True))
        probs_b = probs.astype(BF16)
        dprobs = dot_last(vv, gd)
        delta = jnp.sum(probs_b.astype(F32) * dprobs, axis=0, keepdims=True)
        dscores_b = (probs * (dprobs - delta)).astype(BF16)
        dv = jnp.dot(probs_b, gd, preferred_element_type=F32)
        dk = jnp.dot(dscores_b, qd, preferred_element_type=F32) * scaling
        both = lax.dot_general(dscores_b, kk, CONTRACT_FIRST, preferred_element_type=F32)
        dq[:, start : start + HEAD] = (both[:rows, :HEAD] * scaling).astype(BF16)
        dq[:, start + HEAD : start + wide] = (both[rows:, HEAD:] * scaling).astype(BF16)
        for i, (grad, own) in enumerate(((dk, dk_own), (dv, dv_own))):
            own[:, col] = grad[:rows].astype(BF16)
            mc[i, :, col] = grad[rows : rows + reach].astype(BF16)
            mx[i, :, col] = grad[rows + reach :].astype(BF16)
        if start + wide in store_ends:
            done = (Ellipsis, slice(begin, start + wide))
            for i, (ref, out) in enumerate(zip(held, outs)):
                copies.append(pltpu.make_async_copy(ref.at[done], out.at[done], sems.at[stores, i]))
                copies[-1].start()
            begin, stores = start + wide, stores + 1
    for copy in copies:
        copy.wait()


def attention(bias, query, out_grad, key, value, halo_c, halo_x):
    rows, width = query.shape
    reach = halo_c.shape[1]
    keys = rows + 2 * reach
    twos = width // (2 * HEAD)
    load_ends = sorted({2 * HEAD * n for n in (-(-twos // 5), -(-twos // 2), twos)})
    store_ends = sorted({2 * HEAD * n for n in (-(-twos // 2), -(-twos * 4 // 5), twos)})
    vmem = pl.BlockSpec(memory_space=pltpu.VMEM)
    flat, half = (rows, width), (2, reach, width)
    return pl.pallas_call(
        functools.partial(attention_kernel, load_ends, store_ends),
        in_specs=[vmem]
        + [pl.BlockSpec(memory_space=pltpu.HBM)] * 4
        + [pl.BlockSpec(memory_space=pl.ANY)] * 2,
        out_specs=[pl.BlockSpec(memory_space=pltpu.HBM)] * 5,
        out_shape=[pltpu.HBM(x, BF16) for x in (flat, flat, flat, half, half)],
        scratch_shapes=[pltpu.VMEM(x, BF16) for x in [flat] * 4 + [half] * 2 + [flat] * 3 + [half] * 2]
        + [pltpu.SemaphoreType.DMA((len(load_ends), 6)), pltpu.SemaphoreType.DMA((len(store_ends), 5))],
        cost_estimate=cost(
            20 * rows * keys * width, 22 * width * rows, width // HEAD * rows * keys
        ),
        compiler_params=pltpu.CompilerParams(vmem_limit_bytes=14 << 20),
        name="window_attention",
    )(bias, *far(query, out_grad, key, value), halo_c, halo_x)


def scores_kernel(n_two, scal, k0, q0, *refs):
    paired, received, out = refs[:n_two], refs[n_two : 2 * n_two], refs[2 * n_two]
    local, held, load_sems, sems = refs[2 * n_two + 1 : 3 * n_two + 1], *refs[3 * n_two + 1 :]
    odd = scal[0] % 2
    loads = [
        pltpu.make_async_copy(source, ref, load_sems.at[n])
        for n, (source, ref) in enumerate(zip(received, local))
    ]
    for copy in loads:
        copy.start()

    def work(side):
        arrays = []
        for n in range(n_two):
            both = [(local[n], loads[n]), (paired[n], None)]
            arrays += both[::-1] if side else both
        k1, queries = arrays[0], arrays[1:]
        pairs = [(0, (q0, None), k1)]
        for n in range((held.shape[0] - 1) // 2):
            pairs += [(2 * n + 1, queries[n], (k0, None)), (2 * n + 2, queries[n], k1)]
        pairs.sort(key=lambda pair: sum(load is not None for _, load in pair[1:]))
        copies, waited = [], []
        for n, (q, load_q), (k, load_k) in pairs:
            for load in (load_q, load_k):
                if load is not None and id(load) not in waited:
                    load.wait()
                    waited.append(id(load))
            held[n] = dot_last(q[...], k[...]).astype(BF16)
            copies.append(pltpu.make_async_copy(held.at[n], out.at[n], sems.at[n]))
            copies[-1].start()
        for copy in [load for load in loads if id(load) not in waited] + copies:
            copy.wait()

    pl.when(odd == 0)(functools.partial(work, 0))
    pl.when(odd == 1)(functools.partial(work, 1))


def scores(scal, k0, q0, received, paired, pairs):
    rows, width = k0.shape
    n_two = len(received)
    vmem = pl.BlockSpec(memory_space=pltpu.VMEM)
    hbm = pl.BlockSpec(memory_space=pltpu.HBM)
    anywhere = pl.BlockSpec(memory_space=pl.ANY)
    return pl.pallas_call(
        functools.partial(scores_kernel, n_two),
        in_specs=[pl.BlockSpec(memory_space=pltpu.SMEM)] + [vmem] * (2 + n_two) + [anywhere] * n_two,
        out_specs=hbm,
        out_shape=pltpu.HBM((pairs, rows, rows), BF16),
        scratch_shapes=[pltpu.VMEM((rows, width), BF16)] * n_two
        + [
            pltpu.VMEM((pairs, rows, rows), BF16),
            pltpu.SemaphoreType.DMA((n_two,)),
            pltpu.SemaphoreType.DMA((pairs,)),
        ],
        cost_estimate=cost(20 * 10**9, 2 * pairs * rows * rows),
        compiler_params=room(20, 14 * pairs * rows * rows // 3 + 4 * (1 + n_two) * rows * width),
        name="pair_scores",
    )(scal, k0, q0, *paired, *received)


def rates_kernel(n_far, scal, shares, st, g0, *refs):
    sources, own_out, before_out = refs[:n_far], refs[n_far], refs[n_far + 1]
    held, sems = refs[n_far + 2 : -1], refs[-1]
    f1, moved, f0 = held[0], held[1:-1], held[-1]
    loads = [
        pltpu.make_async_copy(source, ref, sems.at[n])
        for n, (source, ref) in enumerate(zip(sources, held))
    ]
    for copy in loads:
        copy.start()
    lanes = own_out.shape[2]

    def pair(n, g, f):
        products = dot_last(g[...], f[...])
        summed = jnp.sum(st[n].astype(F32) * products, axis=0, keepdims=True)
        return summed * shares[n : n + 1, 0:1]

    loads[0].wait()
    before = pair(0, g0, f1)
    own = jnp.zeros_like(before)
    for n, g in enumerate(moved):
        loads[1 + n].wait()
        before += pair(2 * n + 2, g, f1)
    loads[-1].wait()
    for n, g in enumerate(moved):
        own += pair(2 * n + 1, g, f0)
    for n in range(own_out.shape[0]):
        part = slice(n * lanes, (n + 1) * lanes)
        own_out[n] = own[:, part]
        before_out[n] = before[:, part]


def rates(scal, shares, st, f0, f1, g0, moved, tiles):
    rows, width = f0.shape
    pairs = st.shape[0]
    vmem = pl.BlockSpec(memory_space=pltpu.VMEM)
    n_far = 2 + len(moved)
    return pl.pallas_call(
        functools.partial(rates_kernel, n_far),
        in_specs=[pl.BlockSpec(memory_space=pltpu.SMEM)]
        + [vmem] * 3
        + [pl.BlockSpec(memory_space=pl.ANY)] * (n_far - 1)
        + [pl.BlockSpec(memory_space=pltpu.HBM)],
        out_specs=[vmem] * 2,
        out_shape=[jax.ShapeDtypeStruct((tiles, 1, rows // tiles), F32)] * 2,
        scratch_shapes=[pltpu.VMEM((rows, width), BF16)] * n_far
        + [pltpu.SemaphoreType.DMA((n_far,))],
        cost_estimate=cost(
            2 * pairs * rows * rows * width, 2 * (pairs * rows * rows + (2 + pairs) * rows * width)
        ),
        compiler_params=room(14, (2 * pairs + 16) * rows * rows + 4 * (1 + n_far) * rows * width),
        name="pair_rates",
    )(scal, *near(shares, st, g0), f1, *moved, *far(f0))


def fold_kernel(bit, scal, kept, received, *outs):
    if len(outs) == 1:
        outs[0][...] = (kept[...].astype(F32) + received[...].astype(F32)).astype(kept.dtype)
        return
    keep, send = outs
    side = lax.rem(lax.div(scal[0], 1 << bit), 2)
    for n in range(kept.shape[0]):
        total = (kept[n].astype(F32) + received[n].astype(F32)).astype(kept.dtype)

        def put(ref):
            ref[n // 2] = total

        pl.when(side == n % 2)(functools.partial(put, keep))
        pl.when(side != n % 2)(functools.partial(put, send))


def fold(scal, kept, received, bit):
    vmem = pl.BlockSpec(memory_space=pltpu.VMEM)
    last = kept.shape[0] == 1
    shape = kept.shape if last else (kept.shape[0] // 2, *kept.shape[1:])
    out = jax.ShapeDtypeStruct(shape, kept.dtype)
    return pl.pallas_call(
        functools.partial(fold_kernel, bit),
        in_specs=[pl.BlockSpec(memory_space=pltpu.SMEM), vmem, vmem],
        out_specs=[vmem] if last else [vmem] * 2,
        out_shape=[out] if last else [out] * 2,
        cost_estimate=cost(kept.size, 12 * kept.size),
        compiler_params=room(1, 3 * kept.dtype.itemsize * kept.size + (1 << 20)),
    )(scal, kept, received)


def margins_kernel(parts, scal, dk, dv, mc, mx, *refs):
    outs, (own, core, chip, done), (load_sems, sems) = refs[:2], refs[2:6], refs[6:]
    even = scal[0] % 2 == 0
    reach = mc.shape[1]
    step = dk.shape[1] // parts
    steps = [(i, slice(n * step, (n + 1) * step)) for i in range(2) for n in range(parts)]
    loads, copies = [], []
    for n, (i, cols) in enumerate(steps):
        moves = (
            ((dk, dv)[i].at[:, cols], own.at[i, :, cols]),
            (mc.at[i, :, cols], core.at[i, :, cols]),
            (mx.at[i, :, cols], chip.at[i, :, cols]),
        )
        loads.append([pltpu.make_async_copy(*move, load_sems.at[n, j]) for j, move in enumerate(moves)])
        for copy in loads[-1]:
            copy.start()
    for n, (i, cols) in enumerate(steps):
        for copy in loads[n]:
            copy.wait()
        from_c, from_x = core[i, :, cols].astype(F32), chip[i, :, cols].astype(F32)
        head = jnp.where(even, from_x, from_c)
        tail = jnp.where(even, from_c, from_x)
        done[i, :reach, cols] = (own[i, :reach, cols].astype(F32) + head).astype(BF16)
        done[i, reach:, cols] = (own[i, reach:, cols].astype(F32) + tail).astype(BF16)
        copies.append(pltpu.make_async_copy(done.at[i, :, cols], outs[i].at[:, cols], sems.at[n]))
        copies[-1].start()
    for copy in copies:
        copy.wait()


def add_margins(scal, dk, dv, mc, mx):
    rows, width = dk.shape
    parts = next(n for n in (2, 1) if width % (n * HEAD) == 0)
    hbm = pl.BlockSpec(memory_space=pltpu.HBM)
    whole, half = (2, rows, width), (2, rows // 2, width)
    return pl.pallas_call(
        functools.partial(margins_kernel, parts),
        in_specs=[pl.BlockSpec(memory_space=pltpu.SMEM)]
        + [hbm] * 2
        + [pl.BlockSpec(memory_space=pl.ANY)] * 2,
        out_specs=[hbm] * 2,
        out_shape=[pltpu.HBM((rows, width), BF16)] * 2,
        scratch_shapes=[pltpu.VMEM(x, BF16) for x in (whole, half, half, whole)]
        + [pltpu.SemaphoreType.DMA((2 * parts, 3)), pltpu.SemaphoreType.DMA((2 * parts,))],
        cost_estimate=cost(2 * rows * width, 12 * rows * width),
        compiler_params=pltpu.CompilerParams(vmem_limit_bytes=8 << 20),
        name="add_margins",
    )(scal, *far(dk, dv), mc, mx)


def shifted(array, axis, by):
    devices = lax.axis_size(axis)
    pairs = [(i + by, i) for i in range(devices) if 0 <= i + by < devices]
    return lax.ppermute(array, axis, pairs)


def swapped(array, axis, first):
    devices = lax.axis_size(axis)
    pairs = [(i, i + 1) for i in range(first, devices - 1, 2)]
    return lax.ppermute(array, axis, pairs + [(j, i) for i, j in pairs])


def across(array, axis, bit):
    pairs = [(i, i ^ (1 << bit)) for i in range(lax.axis_size(axis))]
    return lax.ppermute(array, axis, pairs)


def moved_apart(array, by_even, by_odd):
    groups, tiles = lax.axis_size("tm"), lax.axis_size("space")
    pairs = []
    for group in range(groups):
        for tile in range(tiles):
            source = group + (by_odd if tile % 2 else by_even)
            if 0 <= source < groups:
                pairs.append((source * tiles + tile, group * tiles + tile))
    return lax.ppermute(array, ("tm", "space"), pairs)


def per_device(
    attn_query,
    attn_key,
    attn_value,
    attn_outgrad,
    fast_query,
    fast_outgrad,
    fast_key,
    gate_weights,
    up_weights,
    down_weights,
    gate_factor,
    clip_groups,
):
    groups, tiles = lax.axis_size("tm"), lax.axis_size("space")
    scal = lax.axis_index(("tm", "space")).astype(jnp.int32).reshape(1)
    rows = fast_query.shape[0]
    tile_rows, _ = attn_query.shape
    most = groups // 2
    shifts = tuple(range(2, most, 2))
    travels = [-1, *shifts]
    travels += travels[-1:] * (len(travels) % 2)

    outgoing = pick(scal, fast_key, fast_query)
    received = []
    for n in range(0, len(travels), 2):
        array = outgoing if n == 0 else fast_query
        received.append(moved_apart(array, travels[n], travels[n + 1]))
    together = pair_weights(scal, clip_groups, shifts, tiles)
    factor_before = shifted(gate_factor, "tm", -1)
    halo_c, halo_x = pick_halos(scal, attn_key, attn_value)
    halo_c = swapped(halo_c, "space", 0)
    halo_x = swapped(halo_x, "space", 1)

    gate_grad_b, part, sent = fast(
        scal, fast_query, fast_outgrad, gate_weights, up_weights, down_weights, tiles
    )
    for bit in range(tiles.bit_length() - 1):
        arrived = across(sent, "space", bit)
        part, *rest = fold(scal, part, arrived, bit + 1)
        sent = rest[0] if rest else None
    fast_grad = part[0]
    moved = []
    for v in shifts:
        moved.append(shifted(gate_grad_b, "tm", v))

    bias = window_bias(scal, tile_rows, tile_rows // 2, rows)
    dk, dv, query_grad, margin_c, margin_x = attention(
        bias, attn_query, attn_outgrad, attn_key, attn_value, halo_c, halo_x
    )
    margin_c = swapped(margin_c, "space", 0)
    margin_x = swapped(margin_x, "space", 1)

    paired = []
    for array in received:
        paired.append(swapped(array, "space", 0))
    pairs = 1 + 2 * len(shifts)
    st = scores(scal, fast_key, fast_query, received, paired, pairs)
    shares = pair_shares(together, 1.0 / rows)
    own, before = rates(
        scal, shares, st, gate_factor, factor_before, gate_grad_b, moved, tiles
    )
    arrived = shifted(before, "tm", 1)
    key_grad, value_grad = add_margins(scal, dk, dv, margin_c, margin_x)
    kept = own
    for bit in range(tiles.bit_length()):
        kept, *rest = fold(scal, kept, arrived, bit)
        if rest:
            arrived = across(rest[0], "space", bit)
    rate_grad = kept.reshape(-1)
    return query_grad, key_grad, value_grad, fast_grad, rate_grad


def solution(mesh):
    over = ("tm", "space")
    tiled = P(over, None)
    in_specs = (
        (tiled,) * 4
        + (P("tm", None),) * 3
        + (P("tm", None, "space"),) * 2
        + (P("tm", "space", None), P("tm", "space"), P())
    )
    return jax.shard_map(
        per_device,
        mesh=mesh,
        in_specs=in_specs,
        out_specs=(tiled,) * 4 + (P(over),),
        check_vma=False,
    )
```

```python
import functools
import math

import jax
import jax.numpy as jnp
from jax import lax
from jax.experimental import pallas as pl
from jax.experimental.pallas import tpu as pltpu
from jax.sharding import PartitionSpec as P


HEAD = 128

CONTRACT_LAST = (((1,), (1,)), ((), ()))
CONTRACT_FIRST = (((0,), (0,)), ((), ()))
F32 = jnp.float32
BF16 = jnp.bfloat16


def dot_last(a, b):
    return lax.dot_general(a, b, CONTRACT_LAST, preferred_element_type=F32)


def far(*arrays):
    return [pltpu.with_memory_space_constraint(array, pltpu.HBM) for array in arrays]


def near(*arrays):
    return [pltpu.with_memory_space_constraint(array, pltpu.VMEM) for array in arrays]


def room(least, needed):
    return pltpu.CompilerParams(vmem_limit_bytes=max(least << 20, needed))


def cost(flops, moved, transcendentals=0):
    return pl.CostEstimate(flops=flops, bytes_accessed=moved, transcendentals=transcendentals)


def pick_kernel(scal, fk, fq, out, sem):
    odd = scal[0] % 2
    copy = pltpu.make_async_copy(fk, out, sem)
    pl.when(odd == 0)(copy.start)
    pl.when(odd == 1)(pltpu.make_async_copy(fq, out, sem).start)
    copy.wait()


def pick(scal, fast_key, fast_query):
    return pl.pallas_call(
        pick_kernel,
        in_specs=[pl.BlockSpec(memory_space=pltpu.SMEM)]
        + [pl.BlockSpec(memory_space=pltpu.HBM)] * 2,
        out_specs=pl.BlockSpec(memory_space=pltpu.VMEM),
        out_shape=pltpu.VMEM(fast_key.shape, BF16),
        scratch_shapes=[pltpu.SemaphoreType.DMA],
        cost_estimate=cost(0, 4 * fast_key.size),
        compiler_params=pltpu.CompilerParams(vmem_limit_bytes=4 << 20),
        name="pick_outgoing",
    )(scal, *far(fast_key, fast_query))


def halos_kernel(scal, k, v, hc, hx, sems):
    reach = hc.shape[1]
    odd = scal[0] % 2
    copies = []
    for i, source in enumerate((k, v)):
        for j, (half, at) in enumerate(((hx, odd), (hc, 1 - odd))):
            rows = pl.ds(pl.multiple_of(at * reach, reach), reach)
            copies.append(pltpu.make_async_copy(source.at[rows], half.at[i], sems.at[i, j]))
    for copy in copies:
        copy.start()
    for copy in copies:
        copy.wait()


def pick_halos(scal, key, value):
    rows, width = key.shape
    half = jax.ShapeDtypeStruct((2, rows // 2, width), BF16)
    return pl.pallas_call(
        halos_kernel,
        in_specs=[pl.BlockSpec(memory_space=pltpu.SMEM)]
        + [pl.BlockSpec(memory_space=pltpu.HBM)] * 2,
        out_specs=[pl.BlockSpec(memory_space=pltpu.VMEM)] * 2,
        out_shape=[half, half],
        scratch_shapes=[pltpu.SemaphoreType.DMA((2, 2))],
        cost_estimate=cost(0, 8 * rows * width),
        compiler_params=pltpu.CompilerParams(vmem_limit_bytes=4 << 20),
        name="pick_halos",
    )(scal, *far(key, value))


def weights_kernel(shifts, tiles, scal, clips, out):
    at = lax.div(scal[0], tiles)
    starts, total = [], jnp.zeros((1, 1), jnp.int32)
    for n in range(clips.shape[1]):
        starts.append(total)
        total = total + clips[0:1, n : n + 1]
    begins = {}
    for x in range(0, 1 + max((1, *shifts))):
        found = jnp.zeros((1, 1), F32)
        for start in starts:
            found = jnp.maximum(found, jnp.where(start == at + x, 1.0, 0.0))
        begins[x] = found
    for n, (u, v) in enumerate([(1, 0)] + [(u, v) for v in shifts for u in (0, 1)]):
        apart = jnp.zeros((1, 1), F32)
        for x in range(1 - u, v + 1):
            apart = jnp.maximum(apart, begins[x])
        out[n : n + 1, :] = jnp.broadcast_to(1.0 - apart, (1, out.shape[1]))


def pair_weights(scal, clips, shifts, tiles):
    return pl.pallas_call(
        functools.partial(weights_kernel, shifts, tiles),
        in_specs=[
            pl.BlockSpec(memory_space=pltpu.SMEM),
            pl.BlockSpec(memory_space=pltpu.VMEM),
        ],
        out_specs=pl.BlockSpec(memory_space=pltpu.VMEM),
        out_shape=jax.ShapeDtypeStruct((1 + 2 * len(shifts), HEAD), F32),
        cost_estimate=cost(20 * 10**9, 4096),
        compiler_params=pltpu.CompilerParams(vmem_limit_bytes=1 << 20),
        name="pair_weights",
    )(scal, clips.reshape(1, -1))


def fast_kernel(step, ends, scal, q, og, gw, uw, dw, gate_out, keep, send, *refs):
    gate_grad, up_grad, part, gate_sem, sems = refs
    rows = keep.shape[1]
    odd = scal[0] % 2
    for j in range(gw.shape[2] // step):
        cols = slice(j * step, (j + 1) * step)
        gate = jnp.dot(q[...], gw[0, :, cols], preferred_element_type=F32)
        up = jnp.dot(q[...], uw[0, :, cols], preferred_element_type=F32)
        hidden = dot_last(og[...], dw[0, cols, :])
        sig = jax.nn.sigmoid(gate)
        gate_grad[:, cols] = (hidden * up * sig * (1.0 + gate * (1.0 - sig))).astype(BF16)
        up_grad[:, cols] = (hidden * (gate * sig)).astype(BF16)
    copies = [pltpu.make_async_copy(gate_grad, gate_out, gate_sem)]
    copies[0].start()
    begin = 0
    for at in range(0, q.shape[1], step):
        cols = slice(at, at + step)
        part[:, cols] = (
            dot_last(gate_grad[...], gw[0, cols, :]) + dot_last(up_grad[...], uw[0, cols, :])
        ).astype(BF16)
        if at + step in ends:
            cols = slice(begin, at + step)
            for n in range(2 * keep.shape[0]):
                source, sem = part.at[n * rows : (n + 1) * rows, cols], sems.at[ends.index(at + step), n]
                stay = pltpu.make_async_copy(source, keep.at[n // 2, :, cols], sem)
                leave = pltpu.make_async_copy(source, send.at[n // 2, :, cols], sem)
                pl.when(odd == n % 2)(stay.start)
                pl.when(odd != n % 2)(leave.start)
                copies.append(stay)
            begin = at + step
    for copy in copies:
        copy.wait()


def fast(scal, query, outgrad, gate_w, up_w, down_w, tiles):
    rows, width = query.shape
    hidden = gate_w.shape[2]
    step = next(s for s in (256, 128) if hidden % s == 0 and width % s == 0)
    ends = sorted({width // step * 2 // 3 * step, width})
    vmem = pl.BlockSpec(memory_space=pltpu.VMEM)
    half = (tiles // 2, rows // tiles, width)
    return pl.pallas_call(
        functools.partial(fast_kernel, step, ends),
        in_specs=[pl.BlockSpec(memory_space=pltpu.SMEM)] + [vmem] * 5,
        out_specs=[
            pl.BlockSpec(memory_space=pltpu.HBM),
            pl.BlockSpec(memory_space=pl.ANY),
            pl.BlockSpec(memory_space=pltpu.HBM),
        ],
        out_shape=[
            pltpu.HBM((rows, hidden), BF16),
            jax.ShapeDtypeStruct(half, BF16),
            pltpu.HBM(half, BF16),
        ],
        scratch_shapes=[
            pltpu.VMEM((rows, hidden), BF16),
            pltpu.VMEM((rows, hidden), BF16),
            pltpu.VMEM((rows, width), BF16),
            pltpu.SemaphoreType.DMA,
            pltpu.SemaphoreType.DMA((len(ends), tiles)),
        ],
        cost_estimate=cost(20 * 10**9, 6 * width * hidden + 8 * rows * width),
        compiler_params=room(16, (6 * rows * width + 6 * width * hidden + 4 * rows * hidden) * 5 // 4),
        name="fast_weights",
    )(scal, query, outgrad, gate_w, up_w, down_w)


def bias_kernel(reach, last, scal, out):
    keys, rows = out.shape[0], out.shape[1] // 2
    at = lax.rem(scal[0], last // rows)
    even = at % 2 == 0
    key_row = lax.broadcasted_iota(jnp.int32, (keys, rows), 0)
    query_row = lax.broadcasted_iota(jnp.int32, (keys, rows), 1)
    shift_c = jnp.where(even, 0, -(rows + reach))
    shift_x = jnp.where(even, -(rows + 2 * reach), -reach)
    key_pos = key_row + jnp.where(
        key_row < rows, 0, jnp.where(key_row < rows + reach, shift_c, shift_x)
    )
    offset = at * rows
    live = (key_pos + offset >= 0) & (key_pos + offset < last)
    bias = jnp.where(live & (jnp.abs(key_pos - query_row) <= reach), 0.0, -1e30)
    out[:, :rows] = bias
    out[:, rows:] = bias


def share_kernel(share, together, out):
    out[...] = together[...] * share


def pair_shares(together, share):
    vmem = pl.BlockSpec(memory_space=pltpu.VMEM)
    return pl.pallas_call(
        functools.partial(share_kernel, share),
        in_specs=[vmem],
        out_specs=vmem,
        out_shape=jax.ShapeDtypeStruct(together.shape, F32),
        cost_estimate=cost(20 * 10**9, 4096),
        compiler_params=pltpu.CompilerParams(vmem_limit_bytes=1 << 20),
        name="pair_shares",
    )(together)


def window_bias(scal, rows, reach, last):
    return pl.pallas_call(
        functools.partial(bias_kernel, reach, last),
        in_specs=[pl.BlockSpec(memory_space=pltpu.SMEM)],
        out_specs=pl.BlockSpec(memory_space=pltpu.VMEM),
        out_shape=jax.ShapeDtypeStruct((rows + 2 * reach, 2 * rows), F32),
        cost_estimate=cost(20 * 10**9, 16 * rows * rows),
        compiler_params=pltpu.CompilerParams(vmem_limit_bytes=2 << 20),
        name="window_bias",
    )(scal)


def attention_kernel(load_ends, store_ends, bias, *refs):
    sources, outs, local, held = refs[:6], refs[6:11], refs[11:17], refs[17:22]
    load_sems, sems = refs[22:]
    q, g, k, v, hc, hx = local
    dk_own, dv_own, dq, mc, mx = held
    loads, copies = {}, []
    begin = 0
    for n, end in enumerate(load_ends):
        part = (Ellipsis, slice(begin, end))
        loads[begin] = [
            pltpu.make_async_copy(source.at[part], ref.at[part], load_sems.at[n, i])
            for i, (source, ref) in enumerate(zip(sources, local))
        ]
        for copy in loads[begin]:
            copy.start()
        begin = end
    begin, stores = 0, 0
    rows, reach = q.shape[0], hc.shape[1]
    wide = 2 * HEAD
    scaling = 1.0 / math.sqrt(HEAD)
    zero = jnp.zeros((rows, HEAD), BF16)

    def diagonal(ref, at):
        head, other = ref[:, at : at + HEAD], ref[:, at + HEAD : at + wide]
        return jnp.concatenate(
            [jnp.concatenate([head, zero], axis=1), jnp.concatenate([zero, other], axis=1)], axis=0
        )

    for start in range(0, q.shape[1], wide):
        for copy in loads.get(start, ()):
            copy.wait()
        col = slice(start, start + wide)
        kk = jnp.concatenate([k[:, col], hc[0, :, col], hx[0, :, col]], axis=0)
        vv = jnp.concatenate([v[:, col], hc[1, :, col], hx[1, :, col]], axis=0)
        qd, gd = diagonal(q, start), diagonal(g, start)
        scores = dot_last(kk, qd) * scaling + bias[...]
        exponent = jnp.exp(scores - jnp.max(scores, axis=0, keepdims=True))
        probs = exponent * (1.0 / jnp.sum(exponent, axis=0, keepdims=True))
        probs_b = probs.astype(BF16)
        dprobs = dot_last(vv, gd)
        delta = jnp.sum(probs_b.astype(F32) * dprobs, axis=0, keepdims=True)
        dscores_b = (probs * (dprobs - delta)).astype(BF16)
        dv = jnp.dot(probs_b, gd, preferred_element_type=F32)
        dk = jnp.dot(dscores_b, qd, preferred_element_type=F32) * scaling
        both = lax.dot_general(dscores_b, kk, CONTRACT_FIRST, preferred_element_type=F32)
        dq[:, start : start + HEAD] = (both[:rows, :HEAD] * scaling).astype(BF16)
        dq[:, start + HEAD : start + wide] = (both[rows:, HEAD:] * scaling).astype(BF16)
        for i, (grad, own) in enumerate(((dk, dk_own), (dv, dv_own))):
            own[:, col] = grad[:rows].astype(BF16)
            mc[i, :, col] = grad[rows : rows + reach].astype(BF16)
            mx[i, :, col] = grad[rows + reach :].astype(BF16)
        if start + wide in store_ends:
            done = (Ellipsis, slice(begin, start + wide))
            for i, (ref, out) in enumerate(zip(held, outs)):
                copies.append(pltpu.make_async_copy(ref.at[done], out.at[done], sems.at[stores, i]))
                copies[-1].start()
            begin, stores = start + wide, stores + 1
    for copy in copies:
        copy.wait()


def attention(bias, query, out_grad, key, value, halo_c, halo_x):
    rows, width = query.shape
    reach = halo_c.shape[1]
    keys = rows + 2 * reach
    twos = width // (2 * HEAD)
    load_ends = sorted({2 * HEAD * n for n in (-(-twos // 5), -(-twos // 2), twos)})
    store_ends = sorted({2 * HEAD * n for n in (-(-twos // 2), -(-twos * 4 // 5), twos)})
    vmem = pl.BlockSpec(memory_space=pltpu.VMEM)
    flat, half = (rows, width), (2, reach, width)
    return pl.pallas_call(
        functools.partial(attention_kernel, load_ends, store_ends),
        in_specs=[vmem]
        + [pl.BlockSpec(memory_space=pltpu.HBM)] * 4
        + [pl.BlockSpec(memory_space=pl.ANY)] * 2,
        out_specs=[pl.BlockSpec(memory_space=pltpu.HBM)] * 5,
        out_shape=[pltpu.HBM(x, BF16) for x in (flat, flat, flat, half, half)],
        scratch_shapes=[pltpu.VMEM(x, BF16) for x in [flat] * 4 + [half] * 2 + [flat] * 3 + [half] * 2]
        + [pltpu.SemaphoreType.DMA((len(load_ends), 6)), pltpu.SemaphoreType.DMA((len(store_ends), 5))],
        cost_estimate=cost(
            20 * rows * keys * width, 22 * width * rows, width // HEAD * rows * keys
        ),
        compiler_params=pltpu.CompilerParams(vmem_limit_bytes=14 << 20),
        name="window_attention",
    )(bias, *far(query, out_grad, key, value), halo_c, halo_x)


def scores_kernel(n_two, scal, k0, q0, *refs):
    paired, received, out = refs[:n_two], refs[n_two : 2 * n_two], refs[2 * n_two]
    local, held, load_sems, sems = refs[2 * n_two + 1 : 3 * n_two + 1], *refs[3 * n_two + 1 :]
    odd = scal[0] % 2
    loads = [
        pltpu.make_async_copy(source, ref, load_sems.at[n])
        for n, (source, ref) in enumerate(zip(received, local))
    ]
    for copy in loads:
        copy.start()

    def work(side):
        arrays = []
        for n in range(n_two):
            both = [(local[n], loads[n]), (paired[n], None)]
            arrays += both[::-1] if side else both
        k1, queries = arrays[0], arrays[1:]
        pairs = [(0, (q0, None), k1)]
        for n in range((held.shape[0] - 1) // 2):
            pairs += [(2 * n + 1, queries[n], (k0, None)), (2 * n + 2, queries[n], k1)]
        pairs.sort(key=lambda pair: sum(load is not None for _, load in pair[1:]))
        copies, waited = [], []
        for n, (q, load_q), (k, load_k) in pairs:
            for load in (load_q, load_k):
                if load is not None and id(load) not in waited:
                    load.wait()
                    waited.append(id(load))
            held[n] = dot_last(q[...], k[...]).astype(BF16)
            copies.append(pltpu.make_async_copy(held.at[n], out.at[n], sems.at[n]))
            copies[-1].start()
        for copy in [load for load in loads if id(load) not in waited] + copies:
            copy.wait()

    pl.when(odd == 0)(functools.partial(work, 0))
    pl.when(odd == 1)(functools.partial(work, 1))


def scores(scal, k0, q0, received, paired, pairs):
    rows, width = k0.shape
    n_two = len(received)
    vmem = pl.BlockSpec(memory_space=pltpu.VMEM)
    hbm = pl.BlockSpec(memory_space=pltpu.HBM)
    anywhere = pl.BlockSpec(memory_space=pl.ANY)
    return pl.pallas_call(
        functools.partial(scores_kernel, n_two),
        in_specs=[pl.BlockSpec(memory_space=pltpu.SMEM)] + [vmem] * (2 + n_two) + [anywhere] * n_two,
        out_specs=anywhere,
        out_shape=jax.ShapeDtypeStruct((pairs, rows, rows), BF16),
        scratch_shapes=[pltpu.VMEM((rows, width), BF16)] * n_two
        + [
            pltpu.VMEM((pairs, rows, rows), BF16),
            pltpu.SemaphoreType.DMA((n_two,)),
            pltpu.SemaphoreType.DMA((pairs,)),
        ],
        cost_estimate=cost(20 * 10**9, 2 * pairs * rows * rows),
        compiler_params=room(20, 14 * pairs * rows * rows // 3 + 4 * (1 + n_two) * rows * width),
        name="pair_scores",
    )(scal, k0, q0, *paired, *received)


def rates_kernel(n_far, scal, shares, st, g0, *refs):
    sources, own_out, before_out = refs[:n_far], refs[n_far], refs[n_far + 1]
    held, sems = refs[n_far + 2 : -1], refs[-1]
    f1, moved, f0 = held[0], held[1:-1], held[-1]
    loads = [
        pltpu.make_async_copy(source, ref, sems.at[n])
        for n, (source, ref) in enumerate(zip(sources, held))
    ]
    for copy in loads:
        copy.start()
    lanes = own_out.shape[2]

    def pair(n, g, f):
        products = dot_last(g[...], f[...])
        summed = jnp.sum(st[n].astype(F32) * products, axis=0, keepdims=True)
        return summed * shares[n : n + 1, 0:1]

    loads[0].wait()
    before = pair(0, g0, f1)
    own = jnp.zeros_like(before)
    for n, g in enumerate(moved):
        loads[1 + n].wait()
        before += pair(2 * n + 2, g, f1)
    loads[-1].wait()
    for n, g in enumerate(moved):
        own += pair(2 * n + 1, g, f0)
    for n in range(own_out.shape[0]):
        part = slice(n * lanes, (n + 1) * lanes)
        own_out[n] = own[:, part]
        before_out[n] = before[:, part]


def rates(scal, shares, st, f0, f1, g0, moved, tiles):
    rows, width = f0.shape
    pairs = st.shape[0]
    vmem = pl.BlockSpec(memory_space=pltpu.VMEM)
    n_far = 2 + len(moved)
    return pl.pallas_call(
        functools.partial(rates_kernel, n_far),
        in_specs=[pl.BlockSpec(memory_space=pltpu.SMEM)]
        + [vmem] * 3
        + [pl.BlockSpec(memory_space=pl.ANY)] * (n_far - 1)
        + [pl.BlockSpec(memory_space=pltpu.HBM)],
        out_specs=[vmem] * 2,
        out_shape=[jax.ShapeDtypeStruct((tiles, 1, rows // tiles), F32)] * 2,
        scratch_shapes=[pltpu.VMEM((rows, width), BF16)] * n_far
        + [pltpu.SemaphoreType.DMA((n_far,))],
        cost_estimate=cost(
            2 * pairs * rows * rows * width, 2 * (pairs * rows * rows + (2 + pairs) * rows * width)
        ),
        compiler_params=room(14, (2 * pairs + 16) * rows * rows + 4 * (1 + n_far) * rows * width),
        name="pair_rates",
    )(scal, *near(shares, st, g0), f1, *moved, *far(f0))


def fold_kernel(bit, scal, kept, received, *outs):
    if len(outs) == 1:
        outs[0][...] = (kept[...].astype(F32) + received[...].astype(F32)).astype(kept.dtype)
        return
    keep, send = outs
    side = lax.rem(lax.div(scal[0], 1 << bit), 2)
    for n in range(kept.shape[0]):
        total = (kept[n].astype(F32) + received[n].astype(F32)).astype(kept.dtype)

        def put(ref):
            ref[n // 2] = total

        pl.when(side == n % 2)(functools.partial(put, keep))
        pl.when(side != n % 2)(functools.partial(put, send))


def fold(scal, kept, received, bit):
    vmem = pl.BlockSpec(memory_space=pltpu.VMEM)
    last = kept.shape[0] == 1
    shape = kept.shape if last else (kept.shape[0] // 2, *kept.shape[1:])
    out = jax.ShapeDtypeStruct(shape, kept.dtype)
    return pl.pallas_call(
        functools.partial(fold_kernel, bit),
        in_specs=[pl.BlockSpec(memory_space=pltpu.SMEM), vmem, vmem],
        out_specs=[vmem] if last else [vmem] * 2,
        out_shape=[out] if last else [out] * 2,
        cost_estimate=cost(kept.size, 12 * kept.size),
        compiler_params=room(1, 3 * kept.dtype.itemsize * kept.size + (1 << 20)),
    )(scal, kept, received)


def margins_kernel(parts, scal, dk, dv, mc, mx, *refs):
    outs, (own, core, chip, done), (load_sems, sems) = refs[:2], refs[2:6], refs[6:]
    even = scal[0] % 2 == 0
    reach = mc.shape[1]
    step = dk.shape[1] // parts
    steps = [(i, slice(n * step, (n + 1) * step)) for i in range(2) for n in range(parts)]
    loads, copies = [], []
    for n, (i, cols) in enumerate(steps):
        moves = (
            ((dk, dv)[i].at[:, cols], own.at[i, :, cols]),
            (mc.at[i, :, cols], core.at[i, :, cols]),
            (mx.at[i, :, cols], chip.at[i, :, cols]),
        )
        loads.append([pltpu.make_async_copy(*move, load_sems.at[n, j]) for j, move in enumerate(moves)])
        for copy in loads[-1]:
            copy.start()
    for n, (i, cols) in enumerate(steps):
        for copy in loads[n]:
            copy.wait()
        from_c, from_x = core[i, :, cols].astype(F32), chip[i, :, cols].astype(F32)
        head = jnp.where(even, from_x, from_c)
        tail = jnp.where(even, from_c, from_x)
        done[i, :reach, cols] = (own[i, :reach, cols].astype(F32) + head).astype(BF16)
        done[i, reach:, cols] = (own[i, reach:, cols].astype(F32) + tail).astype(BF16)
        copies.append(pltpu.make_async_copy(done.at[i, :, cols], outs[i].at[:, cols], sems.at[n]))
        copies[-1].start()
    for copy in copies:
        copy.wait()


def add_margins(scal, dk, dv, mc, mx):
    rows, width = dk.shape
    parts = next(n for n in (2, 1) if width % (n * HEAD) == 0)
    hbm = pl.BlockSpec(memory_space=pltpu.HBM)
    whole, half = (2, rows, width), (2, rows // 2, width)
    return pl.pallas_call(
        functools.partial(margins_kernel, parts),
        in_specs=[pl.BlockSpec(memory_space=pltpu.SMEM)]
        + [hbm] * 2
        + [pl.BlockSpec(memory_space=pl.ANY)] * 2,
        out_specs=[hbm] * 2,
        out_shape=[pltpu.HBM((rows, width), BF16)] * 2,
        scratch_shapes=[pltpu.VMEM(x, BF16) for x in (whole, half, half, whole)]
        + [pltpu.SemaphoreType.DMA((2 * parts, 3)), pltpu.SemaphoreType.DMA((2 * parts,))],
        cost_estimate=cost(2 * rows * width, 12 * rows * width),
        compiler_params=pltpu.CompilerParams(vmem_limit_bytes=8 << 20),
        name="add_margins",
    )(scal, *far(dk, dv), mc, mx)


def shifted(array, axis, by):
    devices = lax.axis_size(axis)
    pairs = [(i + by, i) for i in range(devices) if 0 <= i + by < devices]
    return lax.ppermute(array, axis, pairs)


def swapped(array, axis, first):
    devices = lax.axis_size(axis)
    pairs = [(i, i + 1) for i in range(first, devices - 1, 2)]
    return lax.ppermute(array, axis, pairs + [(j, i) for i, j in pairs])


def across(array, axis, bit):
    pairs = [(i, i ^ (1 << bit)) for i in range(lax.axis_size(axis))]
    return lax.ppermute(array, axis, pairs)


def moved_apart(array, by_even, by_odd):
    groups, tiles = lax.axis_size("tm"), lax.axis_size("space")
    pairs = []
    for group in range(groups):
        for tile in range(tiles):
            source = group + (by_odd if tile % 2 else by_even)
            if 0 <= source < groups:
                pairs.append((source * tiles + tile, group * tiles + tile))
    return lax.ppermute(array, ("tm", "space"), pairs)


def per_device(
    attn_query,
    attn_key,
    attn_value,
    attn_outgrad,
    fast_query,
    fast_outgrad,
    fast_key,
    gate_weights,
    up_weights,
    down_weights,
    gate_factor,
    clip_groups,
):
    groups, tiles = lax.axis_size("tm"), lax.axis_size("space")
    scal = lax.axis_index(("tm", "space")).astype(jnp.int32).reshape(1)
    rows = fast_query.shape[0]
    tile_rows, _ = attn_query.shape
    most = groups // 2
    shifts = tuple(range(2, most, 2))
    travels = [-1, *shifts]
    travels += travels[-1:] * (len(travels) % 2)

    outgoing = pick(scal, fast_key, fast_query)
    received = []
    for n in range(0, len(travels), 2):
        array = outgoing if n == 0 else fast_query
        received.append(moved_apart(array, travels[n], travels[n + 1]))
    together = pair_weights(scal, clip_groups, shifts, tiles)
    factor_before = shifted(gate_factor, "tm", -1)
    halo_c, halo_x = pick_halos(scal, attn_key, attn_value)
    halo_c = swapped(halo_c, "space", 0)
    halo_x = swapped(halo_x, "space", 1)

    gate_grad_b, part, sent = fast(
        scal, fast_query, fast_outgrad, gate_weights, up_weights, down_weights, tiles
    )
    for bit in range(tiles.bit_length() - 1):
        arrived = across(sent, "space", bit)
        part, *rest = fold(scal, part, arrived, bit + 1)
        sent = rest[0] if rest else None
    fast_grad = part[0]
    moved = []
    for v in shifts:
        moved.append(shifted(gate_grad_b, "tm", v))

    bias = window_bias(scal, tile_rows, tile_rows // 2, rows)
    dk, dv, query_grad, margin_c, margin_x = attention(
        bias, attn_query, attn_outgrad, attn_key, attn_value, halo_c, halo_x
    )
    margin_c = swapped(margin_c, "space", 0)
    margin_x = swapped(margin_x, "space", 1)

    paired = []
    for array in received:
        paired.append(swapped(array, "space", 0))
    pairs = 1 + 2 * len(shifts)
    st = scores(scal, fast_key, fast_query, received, paired, pairs)
    shares = pair_shares(together, 1.0 / rows)
    own, before = rates(
        scal, shares, st, gate_factor, factor_before, gate_grad_b, moved, tiles
    )
    arrived = shifted(before, "tm", 1)
    key_grad, value_grad = add_margins(scal, dk, dv, margin_c, margin_x)
    kept = own
    for bit in range(tiles.bit_length()):
        kept, *rest = fold(scal, kept, arrived, bit)
        if rest:
            arrived = across(rest[0], "space", bit)
    rate_grad = kept.reshape(-1)
    return query_grad, key_grad, value_grad, fast_grad, rate_grad


def solution(mesh):
    over = ("tm", "space")
    tiled = P(over, None)
    in_specs = (
        (tiled,) * 4
        + (P("tm", None),) * 3
        + (P("tm", None, "space"),) * 2
        + (P("tm", "space", None), P("tm", "space"), P())
    )
    return jax.shard_map(
        per_device,
        mesh=mesh,
        in_specs=in_specs,
        out_specs=(tiled,) * 4 + (P(over),),
        check_vma=False,
    )
```

```python
import functools
import math

import jax
import jax.numpy as jnp
from jax import lax
from jax.experimental import pallas as pl
from jax.experimental.pallas import tpu as pltpu
from jax.sharding import PartitionSpec as P


HEAD = 128

CONTRACT_LAST = (((1,), (1,)), ((), ()))
CONTRACT_FIRST = (((0,), (0,)), ((), ()))
F32 = jnp.float32
BF16 = jnp.bfloat16


def dot_last(a, b):
    return lax.dot_general(a, b, CONTRACT_LAST, preferred_element_type=F32)


def far(*arrays):
    return [pltpu.with_memory_space_constraint(array, pltpu.HBM) for array in arrays]


def near(*arrays):
    return [pltpu.with_memory_space_constraint(array, pltpu.VMEM) for array in arrays]


def room(least, needed):
    return pltpu.CompilerParams(vmem_limit_bytes=max(least << 20, needed))


def cost(flops, moved, transcendentals=0):
    return pl.CostEstimate(flops=flops, bytes_accessed=moved, transcendentals=transcendentals)


def pick_kernel(scal, fk, fq, out, sem):
    odd = scal[0] % 2
    copy = pltpu.make_async_copy(fk, out, sem)
    pl.when(odd == 0)(copy.start)
    pl.when(odd == 1)(pltpu.make_async_copy(fq, out, sem).start)
    copy.wait()


def pick(scal, fast_key, fast_query):
    return pl.pallas_call(
        pick_kernel,
        in_specs=[pl.BlockSpec(memory_space=pltpu.SMEM)]
        + [pl.BlockSpec(memory_space=pltpu.HBM)] * 2,
        out_specs=pl.BlockSpec(memory_space=pltpu.VMEM),
        out_shape=pltpu.VMEM(fast_key.shape, BF16),
        scratch_shapes=[pltpu.SemaphoreType.DMA],
        cost_estimate=cost(0, 4 * fast_key.size),
        compiler_params=pltpu.CompilerParams(vmem_limit_bytes=4 << 20),
        name="pick_outgoing",
    )(scal, *far(fast_key, fast_query))


def halos_kernel(scal, k, v, hc, hx, sems):
    reach = hc.shape[1]
    odd = scal[0] % 2
    copies = []
    for i, source in enumerate((k, v)):
        for j, (half, at) in enumerate(((hx, odd), (hc, 1 - odd))):
            rows = pl.ds(pl.multiple_of(at * reach, reach), reach)
            copies.append(pltpu.make_async_copy(source.at[rows], half.at[i], sems.at[i, j]))
    for copy in copies:
        copy.start()
    for copy in copies:
        copy.wait()


def pick_halos(scal, key, value):
    rows, width = key.shape
    half = jax.ShapeDtypeStruct((2, rows // 2, width), BF16)
    return pl.pallas_call(
        halos_kernel,
        in_specs=[pl.BlockSpec(memory_space=pltpu.SMEM)]
        + [pl.BlockSpec(memory_space=pltpu.HBM)] * 2,
        out_specs=[pl.BlockSpec(memory_space=pltpu.VMEM)] * 2,
        out_shape=[half, half],
        scratch_shapes=[pltpu.SemaphoreType.DMA((2, 2))],
        cost_estimate=cost(0, 8 * rows * width),
        compiler_params=pltpu.CompilerParams(vmem_limit_bytes=4 << 20),
        name="pick_halos",
    )(scal, *far(key, value))


def weights_kernel(shifts, tiles, scal, clips, out):
    at = lax.div(scal[0], tiles)
    starts, total = [], jnp.zeros((1, 1), jnp.int32)
    for n in range(clips.shape[1]):
        starts.append(total)
        total = total + clips[0:1, n : n + 1]
    begins = {}
    for x in range(0, 1 + max((1, *shifts))):
        found = jnp.zeros((1, 1), F32)
        for start in starts:
            found = jnp.maximum(found, jnp.where(start == at + x, 1.0, 0.0))
        begins[x] = found
    for n, (u, v) in enumerate([(1, 0)] + [(u, v) for v in shifts for u in (0, 1)]):
        apart = jnp.zeros((1, 1), F32)
        for x in range(1 - u, v + 1):
            apart = jnp.maximum(apart, begins[x])
        out[n : n + 1, :] = jnp.broadcast_to(1.0 - apart, (1, out.shape[1]))


def pair_weights(scal, clips, shifts, tiles):
    return pl.pallas_call(
        functools.partial(weights_kernel, shifts, tiles),
        in_specs=[
            pl.BlockSpec(memory_space=pltpu.SMEM),
            pl.BlockSpec(memory_space=pltpu.VMEM),
        ],
        out_specs=pl.BlockSpec(memory_space=pltpu.VMEM),
        out_shape=jax.ShapeDtypeStruct((1 + 2 * len(shifts), HEAD), F32),
        cost_estimate=cost(20 * 10**9, 4096),
        compiler_params=pltpu.CompilerParams(vmem_limit_bytes=1 << 20),
        name="pair_weights",
    )(scal, clips.reshape(1, -1))


def fast_kernel(step, ends, scal, q, og, gw, uw, dw, gate_out, keep, send, *refs):
    gate_grad, up_grad, part, gate_sem, sems = refs
    rows = keep.shape[1]
    odd = scal[0] % 2
    for j in range(gw.shape[2] // step):
        cols = slice(j * step, (j + 1) * step)
        gate = jnp.dot(q[...], gw[0, :, cols], preferred_element_type=F32)
        up = jnp.dot(q[...], uw[0, :, cols], preferred_element_type=F32)
        hidden = dot_last(og[...], dw[0, cols, :])
        sig = jax.nn.sigmoid(gate)
        gate_grad[:, cols] = (hidden * up * sig * (1.0 + gate * (1.0 - sig))).astype(BF16)
        up_grad[:, cols] = (hidden * (gate * sig)).astype(BF16)
    copies = [pltpu.make_async_copy(gate_grad, gate_out, gate_sem)]
    copies[0].start()
    begin = 0
    for at in range(0, q.shape[1], step):
        cols = slice(at, at + step)
        part[:, cols] = (
            dot_last(gate_grad[...], gw[0, cols, :]) + dot_last(up_grad[...], uw[0, cols, :])
        ).astype(BF16)
        if at + step in ends:
            cols = slice(begin, at + step)
            for n in range(2 * keep.shape[0]):
                source, sem = part.at[n * rows : (n + 1) * rows, cols], sems.at[ends.index(at + step), n]
                stay = pltpu.make_async_copy(source, keep.at[n // 2, :, cols], sem)
                leave = pltpu.make_async_copy(source, send.at[n // 2, :, cols], sem)
                pl.when(odd == n % 2)(stay.start)
                pl.when(odd != n % 2)(leave.start)
                copies.append(stay)
            begin = at + step
    for copy in copies:
        copy.wait()


def fast(scal, query, outgrad, gate_w, up_w, down_w, tiles):
    rows, width = query.shape
    hidden = gate_w.shape[2]
    step = next(s for s in (256, 128) if hidden % s == 0 and width % s == 0)
    ends = sorted({width // step * 2 // 3 * step, width})
    vmem = pl.BlockSpec(memory_space=pltpu.VMEM)
    half = (tiles // 2, rows // tiles, width)
    return pl.pallas_call(
        functools.partial(fast_kernel, step, ends),
        in_specs=[pl.BlockSpec(memory_space=pltpu.SMEM)] + [vmem] * 5,
        out_specs=[
            pl.BlockSpec(memory_space=pltpu.HBM),
            pl.BlockSpec(memory_space=pl.ANY),
            pl.BlockSpec(memory_space=pltpu.HBM),
        ],
        out_shape=[
            pltpu.HBM((rows, hidden), BF16),
            jax.ShapeDtypeStruct(half, BF16),
            pltpu.HBM(half, BF16),
        ],
        scratch_shapes=[
            pltpu.VMEM((rows, hidden), BF16),
            pltpu.VMEM((rows, hidden), BF16),
            pltpu.VMEM((rows, width), BF16),
            pltpu.SemaphoreType.DMA,
            pltpu.SemaphoreType.DMA((len(ends), tiles)),
        ],
        cost_estimate=cost(20 * 10**9, 6 * width * hidden + 8 * rows * width),
        compiler_params=room(16, (6 * rows * width + 6 * width * hidden + 4 * rows * hidden) * 5 // 4),
        name="fast_weights",
    )(scal, query, outgrad, gate_w, up_w, down_w)


def bias_kernel(reach, last, scal, out):
    keys, rows = out.shape[0], out.shape[1] // 2
    at = lax.rem(scal[0], last // rows)
    even = at % 2 == 0
    key_row = lax.broadcasted_iota(jnp.int32, (keys, rows), 0)
    query_row = lax.broadcasted_iota(jnp.int32, (keys, rows), 1)
    shift_c = jnp.where(even, 0, -(rows + reach))
    shift_x = jnp.where(even, -(rows + 2 * reach), -reach)
    key_pos = key_row + jnp.where(
        key_row < rows, 0, jnp.where(key_row < rows + reach, shift_c, shift_x)
    )
    offset = at * rows
    live = (key_pos + offset >= 0) & (key_pos + offset < last)
    bias = jnp.where(live & (jnp.abs(key_pos - query_row) <= reach), 0.0, -1e30)
    out[:, :rows] = bias
    out[:, rows:] = bias


def share_kernel(share, together, out):
    out[...] = together[...] * share


def pair_shares(together, share):
    vmem = pl.BlockSpec(memory_space=pltpu.VMEM)
    return pl.pallas_call(
        functools.partial(share_kernel, share),
        in_specs=[vmem],
        out_specs=vmem,
        out_shape=jax.ShapeDtypeStruct(together.shape, F32),
        cost_estimate=cost(20 * 10**9, 4096),
        compiler_params=pltpu.CompilerParams(vmem_limit_bytes=1 << 20),
        name="pair_shares",
    )(together)


def window_bias(scal, rows, reach, last):
    return pl.pallas_call(
        functools.partial(bias_kernel, reach, last),
        in_specs=[pl.BlockSpec(memory_space=pltpu.SMEM)],
        out_specs=pl.BlockSpec(memory_space=pltpu.VMEM),
        out_shape=jax.ShapeDtypeStruct((rows + 2 * reach, 2 * rows), F32),
        cost_estimate=cost(20 * 10**9, 16 * rows * rows),
        compiler_params=pltpu.CompilerParams(vmem_limit_bytes=2 << 20),
        name="window_bias",
    )(scal)


def attention_kernel(load_ends, store_ends, bias, *refs):
    sources, outs, local, held = refs[:6], refs[6:11], refs[11:17], refs[17:22]
    load_sems, sems = refs[22:]
    q, g, k, v, hc, hx = local
    dk_own, dv_own, dq, mc, mx = held
    loads, copies = {}, []
    begin = 0
    for n, end in enumerate(load_ends):
        part = (Ellipsis, slice(begin, end))
        loads[begin] = [
            pltpu.make_async_copy(source.at[part], ref.at[part], load_sems.at[n, i])
            for i, (source, ref) in enumerate(zip(sources, local))
        ]
        for copy in loads[begin]:
            copy.start()
        begin = end
    begin, stores = 0, 0
    rows, reach = q.shape[0], hc.shape[1]
    wide = 2 * HEAD
    scaling = 1.0 / math.sqrt(HEAD)
    zero = jnp.zeros((rows, HEAD), BF16)

    def diagonal(ref, at):
        head, other = ref[:, at : at + HEAD], ref[:, at + HEAD : at + wide]
        return jnp.concatenate(
            [jnp.concatenate([head, zero], axis=1), jnp.concatenate([zero, other], axis=1)], axis=0
        )

    for start in range(0, q.shape[1], wide):
        for copy in loads.get(start, ()):
            copy.wait()
        col = slice(start, start + wide)
        kk = jnp.concatenate([k[:, col], hc[0, :, col], hx[0, :, col]], axis=0)
        vv = jnp.concatenate([v[:, col], hc[1, :, col], hx[1, :, col]], axis=0)
        qd, gd = diagonal(q, start), diagonal(g, start)
        scores = dot_last(kk, qd) * scaling + bias[...]
        exponent = jnp.exp(scores - jnp.max(scores, axis=0, keepdims=True))
        probs = exponent * (1.0 / jnp.sum(exponent, axis=0, keepdims=True))
        probs_b = probs.astype(BF16)
        dprobs = dot_last(vv, gd)
        delta = jnp.sum(probs_b.astype(F32) * dprobs, axis=0, keepdims=True)
        dscores_b = (probs * (dprobs - delta)).astype(BF16)
        dv = jnp.dot(probs_b, gd, preferred_element_type=F32)
        dk = jnp.dot(dscores_b, qd, preferred_element_type=F32) * scaling
        both = lax.dot_general(dscores_b, kk, CONTRACT_FIRST, preferred_element_type=F32)
        dq[:, start : start + HEAD] = (both[:rows, :HEAD] * scaling).astype(BF16)
        dq[:, start + HEAD : start + wide] = (both[rows:, HEAD:] * scaling).astype(BF16)
        for i, (grad, own) in enumerate(((dk, dk_own), (dv, dv_own))):
            own[:, col] = grad[:rows].astype(BF16)
            mc[i, :, col] = grad[rows : rows + reach].astype(BF16)
            mx[i, :, col] = grad[rows + reach :].astype(BF16)
        if start + wide in store_ends:
            done = (Ellipsis, slice(begin, start + wide))
            for i, (ref, out) in enumerate(zip(held, outs)):
                copies.append(pltpu.make_async_copy(ref.at[done], out.at[done], sems.at[stores, i]))
                copies[-1].start()
            begin, stores = start + wide, stores + 1
    for copy in copies:
        copy.wait()


def attention(bias, query, out_grad, key, value, halo_c, halo_x):
    rows, width = query.shape
    reach = halo_c.shape[1]
    keys = rows + 2 * reach
    twos = width // (2 * HEAD)
    load_ends = sorted({2 * HEAD * n for n in (-(-twos // 5), -(-twos // 2), twos)})
    store_ends = sorted({2 * HEAD * n for n in (-(-twos // 2), -(-twos * 4 // 5), twos)})
    vmem = pl.BlockSpec(memory_space=pltpu.VMEM)
    flat, half = (rows, width), (2, reach, width)
    return pl.pallas_call(
        functools.partial(attention_kernel, load_ends, store_ends),
        in_specs=[vmem]
        + [pl.BlockSpec(memory_space=pltpu.HBM)] * 4
        + [pl.BlockSpec(memory_space=pl.ANY)] * 2,
        out_specs=[pl.BlockSpec(memory_space=pl.ANY)] * 2
        + [pl.BlockSpec(memory_space=pltpu.HBM)] * 3,
        out_shape=[jax.ShapeDtypeStruct(flat, BF16)] * 2
        + [pltpu.HBM(x, BF16) for x in (flat, half, half)],
        scratch_shapes=[pltpu.VMEM(x, BF16) for x in [flat] * 4 + [half] * 2 + [flat] * 3 + [half] * 2]
        + [pltpu.SemaphoreType.DMA((len(load_ends), 6)), pltpu.SemaphoreType.DMA((len(store_ends), 5))],
        cost_estimate=cost(
            20 * rows * keys * width, 22 * width * rows, width // HEAD * rows * keys
        ),
        compiler_params=pltpu.CompilerParams(vmem_limit_bytes=14 << 20),
        name="window_attention",
    )(bias, *far(query, out_grad, key, value), halo_c, halo_x)


def scores_kernel(n_two, scal, k0, q0, *refs):
    paired, received, out = refs[:n_two], refs[n_two : 2 * n_two], refs[2 * n_two]
    local, held, load_sems, sems = refs[2 * n_two + 1 : 3 * n_two + 1], *refs[3 * n_two + 1 :]
    odd = scal[0] % 2
    loads = [
        pltpu.make_async_copy(source, ref, load_sems.at[n])
        for n, (source, ref) in enumerate(zip(received, local))
    ]
    for copy in loads:
        copy.start()

    def work(side):
        arrays = []
        for n in range(n_two):
            both = [(local[n], loads[n]), (paired[n], None)]
            arrays += both[::-1] if side else both
        k1, queries = arrays[0], arrays[1:]
        pairs = [(0, (q0, None), k1)]
        for n in range((held.shape[0] - 1) // 2):
            pairs += [(2 * n + 1, queries[n], (k0, None)), (2 * n + 2, queries[n], k1)]
        pairs.sort(key=lambda pair: sum(load is not None for _, load in pair[1:]))
        copies, waited = [], []
        for n, (q, load_q), (k, load_k) in pairs:
            for load in (load_q, load_k):
                if load is not None and id(load) not in waited:
                    load.wait()
                    waited.append(id(load))
            held[n] = dot_last(q[...], k[...]).astype(BF16)
            copies.append(pltpu.make_async_copy(held.at[n], out.at[n], sems.at[n]))
            copies[-1].start()
        for copy in [load for load in loads if id(load) not in waited] + copies:
            copy.wait()

    pl.when(odd == 0)(functools.partial(work, 0))
    pl.when(odd == 1)(functools.partial(work, 1))


def scores(scal, k0, q0, received, paired, pairs):
    rows, width = k0.shape
    n_two = len(received)
    vmem = pl.BlockSpec(memory_space=pltpu.VMEM)
    hbm = pl.BlockSpec(memory_space=pltpu.HBM)
    anywhere = pl.BlockSpec(memory_space=pl.ANY)
    return pl.pallas_call(
        functools.partial(scores_kernel, n_two),
        in_specs=[pl.BlockSpec(memory_space=pltpu.SMEM)] + [vmem] * (2 + n_two) + [anywhere] * n_two,
        out_specs=anywhere,
        out_shape=jax.ShapeDtypeStruct((pairs, rows, rows), BF16),
        scratch_shapes=[pltpu.VMEM((rows, width), BF16)] * n_two
        + [
            pltpu.VMEM((pairs, rows, rows), BF16),
            pltpu.SemaphoreType.DMA((n_two,)),
            pltpu.SemaphoreType.DMA((pairs,)),
        ],
        cost_estimate=cost(20 * 10**9, 2 * pairs * rows * rows),
        compiler_params=room(20, 14 * pairs * rows * rows // 3 + 4 * (1 + n_two) * rows * width),
        name="pair_scores",
    )(scal, k0, q0, *paired, *received)


def rates_kernel(n_far, scal, shares, st, g0, *refs):
    sources, own_out, before_out = refs[:n_far], refs[n_far], refs[n_far + 1]
    held, sems = refs[n_far + 2 : -1], refs[-1]
    f1, moved, f0 = held[0], held[1:-1], held[-1]
    loads = [
        pltpu.make_async_copy(source, ref, sems.at[n])
        for n, (source, ref) in enumerate(zip(sources, held))
    ]
    for copy in loads:
        copy.start()
    lanes = own_out.shape[2]

    def pair(n, g, f):
        products = dot_last(g[...], f[...])
        summed = jnp.sum(st[n].astype(F32) * products, axis=0, keepdims=True)
        return summed * shares[n : n + 1, 0:1]

    loads[0].wait()
    before = pair(0, g0, f1)
    own = jnp.zeros_like(before)
    for n, g in enumerate(moved):
        loads[1 + n].wait()
        before += pair(2 * n + 2, g, f1)
    loads[-1].wait()
    for n, g in enumerate(moved):
        own += pair(2 * n + 1, g, f0)
    for n in range(own_out.shape[0]):
        part = slice(n * lanes, (n + 1) * lanes)
        own_out[n] = own[:, part]
        before_out[n] = before[:, part]


def rates(scal, shares, st, f0, f1, g0, moved, tiles):
    rows, width = f0.shape
    pairs = st.shape[0]
    vmem = pl.BlockSpec(memory_space=pltpu.VMEM)
    n_far = 2 + len(moved)
    return pl.pallas_call(
        functools.partial(rates_kernel, n_far),
        in_specs=[pl.BlockSpec(memory_space=pltpu.SMEM)]
        + [vmem] * 3
        + [pl.BlockSpec(memory_space=pl.ANY)] * (n_far - 1)
        + [pl.BlockSpec(memory_space=pltpu.HBM)],
        out_specs=[vmem] * 2,
        out_shape=[jax.ShapeDtypeStruct((tiles, 1, rows // tiles), F32)] * 2,
        scratch_shapes=[pltpu.VMEM((rows, width), BF16)] * n_far
        + [pltpu.SemaphoreType.DMA((n_far,))],
        cost_estimate=cost(
            2 * pairs * rows * rows * width, 2 * (pairs * rows * rows + (2 + pairs) * rows * width)
        ),
        compiler_params=room(14, (2 * pairs + 16) * rows * rows + 4 * (1 + n_far) * rows * width),
        name="pair_rates",
    )(scal, *near(shares, st, g0), f1, *moved, *far(f0))


def fold_kernel(bit, scal, kept, received, *outs):
    if len(outs) == 1:
        outs[0][...] = (kept[...].astype(F32) + received[...].astype(F32)).astype(kept.dtype)
        return
    keep, send = outs
    side = lax.rem(lax.div(scal[0], 1 << bit), 2)
    for n in range(kept.shape[0]):
        total = (kept[n].astype(F32) + received[n].astype(F32)).astype(kept.dtype)

        def put(ref):
            ref[n // 2] = total

        pl.when(side == n % 2)(functools.partial(put, keep))
        pl.when(side != n % 2)(functools.partial(put, send))


def fold(scal, kept, received, bit):
    vmem = pl.BlockSpec(memory_space=pltpu.VMEM)
    last = kept.shape[0] == 1
    shape = kept.shape if last else (kept.shape[0] // 2, *kept.shape[1:])
    out = jax.ShapeDtypeStruct(shape, kept.dtype)
    return pl.pallas_call(
        functools.partial(fold_kernel, bit),
        in_specs=[pl.BlockSpec(memory_space=pltpu.SMEM), vmem, vmem],
        out_specs=[vmem] if last else [vmem] * 2,
        out_shape=[out] if last else [out] * 2,
        cost_estimate=cost(kept.size, 12 * kept.size),
        compiler_params=room(1, 3 * kept.dtype.itemsize * kept.size + (1 << 20)),
    )(scal, kept, received)


def margins_kernel(parts, scal, dk, dv, mc, mx, *refs):
    outs, (own, core, chip, done), (load_sems, sems) = refs[:2], refs[2:6], refs[6:]
    even = scal[0] % 2 == 0
    reach = mc.shape[1]
    step = dk.shape[1] // parts
    steps = [(i, slice(n * step, (n + 1) * step)) for i in range(2) for n in range(parts)]
    loads, copies = [], []
    for n, (i, cols) in enumerate(steps):
        moves = (
            ((dk, dv)[i].at[:, cols], own.at[i, :, cols]),
            (mc.at[i, :, cols], core.at[i, :, cols]),
            (mx.at[i, :, cols], chip.at[i, :, cols]),
        )
        loads.append([pltpu.make_async_copy(*move, load_sems.at[n, j]) for j, move in enumerate(moves)])
        for copy in loads[-1]:
            copy.start()
    for n, (i, cols) in enumerate(steps):
        for copy in loads[n]:
            copy.wait()
        from_c, from_x = core[i, :, cols].astype(F32), chip[i, :, cols].astype(F32)
        head = jnp.where(even, from_x, from_c)
        tail = jnp.where(even, from_c, from_x)
        done[i, :reach, cols] = (own[i, :reach, cols].astype(F32) + head).astype(BF16)
        done[i, reach:, cols] = (own[i, reach:, cols].astype(F32) + tail).astype(BF16)
        copies.append(pltpu.make_async_copy(done.at[i, :, cols], outs[i].at[:, cols], sems.at[n]))
        copies[-1].start()
    for copy in copies:
        copy.wait()


def add_margins(scal, dk, dv, mc, mx):
    rows, width = dk.shape
    parts = next(n for n in (2, 1) if width % (n * HEAD) == 0)
    hbm = pl.BlockSpec(memory_space=pltpu.HBM)
    whole, half = (2, rows, width), (2, rows // 2, width)
    return pl.pallas_call(
        functools.partial(margins_kernel, parts),
        in_specs=[pl.BlockSpec(memory_space=pltpu.SMEM)]
        + [pl.BlockSpec(memory_space=pl.ANY)] * 4,
        out_specs=[hbm] * 2,
        out_shape=[pltpu.HBM((rows, width), BF16)] * 2,
        scratch_shapes=[pltpu.VMEM(x, BF16) for x in (whole, half, half, whole)]
        + [pltpu.SemaphoreType.DMA((2 * parts, 3)), pltpu.SemaphoreType.DMA((2 * parts,))],
        cost_estimate=cost(2 * rows * width, 12 * rows * width),
        compiler_params=pltpu.CompilerParams(vmem_limit_bytes=8 << 20),
        name="add_margins",
    )(scal, dk, dv, mc, mx)


def shifted(array, axis, by):
    devices = lax.axis_size(axis)
    pairs = [(i + by, i) for i in range(devices) if 0 <= i + by < devices]
    return lax.ppermute(array, axis, pairs)


def swapped(array, axis, first):
    devices = lax.axis_size(axis)
    pairs = [(i, i + 1) for i in range(first, devices - 1, 2)]
    return lax.ppermute(array, axis, pairs + [(j, i) for i, j in pairs])


def across(array, axis, bit):
    pairs = [(i, i ^ (1 << bit)) for i in range(lax.axis_size(axis))]
    return lax.ppermute(array, axis, pairs)


def moved_apart(array, by_even, by_odd):
    groups, tiles = lax.axis_size("tm"), lax.axis_size("space")
    pairs = []
    for group in range(groups):
        for tile in range(tiles):
            source = group + (by_odd if tile % 2 else by_even)
            if 0 <= source < groups:
                pairs.append((source * tiles + tile, group * tiles + tile))
    return lax.ppermute(array, ("tm", "space"), pairs)


def per_device(
    attn_query,
    attn_key,
    attn_value,
    attn_outgrad,
    fast_query,
    fast_outgrad,
    fast_key,
    gate_weights,
    up_weights,
    down_weights,
    gate_factor,
    clip_groups,
):
    groups, tiles = lax.axis_size("tm"), lax.axis_size("space")
    scal = lax.axis_index(("tm", "space")).astype(jnp.int32).reshape(1)
    rows = fast_query.shape[0]
    tile_rows, _ = attn_query.shape
    most = groups // 2
    shifts = tuple(range(2, most, 2))
    travels = [-1, *shifts]
    travels += travels[-1:] * (len(travels) % 2)

    outgoing = pick(scal, fast_key, fast_query)
    received = []
    for n in range(0, len(travels), 2):
        array = outgoing if n == 0 else fast_query
        received.append(moved_apart(array, travels[n], travels[n + 1]))
    together = pair_weights(scal, clip_groups, shifts, tiles)
    factor_before = shifted(gate_factor, "tm", -1)
    halo_c, halo_x = pick_halos(scal, attn_key, attn_value)
    halo_c = swapped(halo_c, "space", 0)
    halo_x = swapped(halo_x, "space", 1)

    gate_grad_b, part, sent = fast(
        scal, fast_query, fast_outgrad, gate_weights, up_weights, down_weights, tiles
    )
    for bit in range(tiles.bit_length() - 1):
        arrived = across(sent, "space", bit)
        part, *rest = fold(scal, part, arrived, bit + 1)
        sent = rest[0] if rest else None
    fast_grad = part[0]
    moved = []
    for v in shifts:
        moved.append(shifted(gate_grad_b, "tm", v))

    bias = window_bias(scal, tile_rows, tile_rows // 2, rows)
    dk, dv, query_grad, margin_c, margin_x = attention(
        bias, attn_query, attn_outgrad, attn_key, attn_value, halo_c, halo_x
    )
    margin_c = swapped(margin_c, "space", 0)
    margin_x = swapped(margin_x, "space", 1)

    paired = []
    for array in received:
        paired.append(swapped(array, "space", 0))
    pairs = 1 + 2 * len(shifts)
    st = scores(scal, fast_key, fast_query, received, paired, pairs)
    shares = pair_shares(together, 1.0 / rows)
    own, before = rates(
        scal, shares, st, gate_factor, factor_before, gate_grad_b, moved, tiles
    )
    arrived = shifted(before, "tm", 1)
    key_grad, value_grad = add_margins(scal, dk, dv, margin_c, margin_x)
    kept = own
    for bit in range(tiles.bit_length()):
        kept, *rest = fold(scal, kept, arrived, bit)
        if rest:
            arrived = across(rest[0], "space", bit)
    rate_grad = kept.reshape(-1)
    return query_grad, key_grad, value_grad, fast_grad, rate_grad


def solution(mesh):
    over = ("tm", "space")
    tiled = P(over, None)
    in_specs = (
        (tiled,) * 4
        + (P("tm", None),) * 3
        + (P("tm", None, "space"),) * 2
        + (P("tm", "space", None), P("tm", "space"), P())
    )
    return jax.shard_map(
        per_device,
        mesh=mesh,
        in_specs=in_specs,
        out_specs=(tiled,) * 4 + (P(over),),
        check_vma=False,
    )
```
